32 devices in a mesh: branch: 2 (over x), strip: 16 (over z, y, core).
Axes of the slice: x: 2, y: 2, z: 4, core: 2. Of those that a mesh axis runs over, the one named last changes fastest.
Arguments:
- image_feats: bfloat16 [32, 2048, 256], P(None, ('branch', 'strip')), may hold values from -6 to 6
- cam_weights: bfloat16 [3, 9, 256, 256], replicated, may hold values from -0.1875 to 0.1875
- depth_weight: bfloat16 [256, 118], replicated, may hold values from -1.5 to 1.5
- ray_bins: int32 [2048, 118], P(('branch', 'strip')), may hold values from 0 to 2047, as said below
- pillar_sums: bfloat16 [32, 256, 128], P(None, ('branch', 'strip')), may hold values from -12 to 12
- pillar_counts: int32 [32, 256], P(None, ('branch', 'strip')), may hold values from 0 to 8
- lidar_weight: bfloat16 [4, 128, 128], replicated, may hold values from -0.375 to 0.375
- merge_weight: bfloat16 [9, 384, 256], replicated, may hold values from -0.15625 to 0.15625
- out_cotangent: bfloat16 [16, 128, 256], P(None, ('branch', 'strip')), may hold values from -6 to 6
Outputs:
- merged: bfloat16 [16, 128, 256], P(None, ('branch', 'strip'))
- cam_grad: bfloat16 [32, 2048, 256], P(None, ('branch', 'strip'))
- lid_grad: bfloat16 [16, 128, 128], P(None, ('branch', 'strip'))
The draws below stay inside these ranges and needn't reach their ends.
Inputs may be any that keep to these rules, and one draw needn't show every extreme that they name: For a column j of sector s = j // 64, ray_bins[j, k] lies in sector s - 1, s or s + 1 taken modulo 32, in cycle k * 16 // 118.
All inputs are finite; a program needn't handle non-finite values.
Results may differ from the reference program's by a relative error of at most 0.014.
Values may be sent and summed in bfloat16 or wider, within the bound.
A program may use at most 128 MiB of HBM per device.

```python
import jax
import jax.numpy as jnp
from jax import lax

C = 256
CL = 128
CF = 256
DB = 118
ROWS = 32
LAYERS = 3
COLS_DEV = 64
BR = 16
BA = 4
NSECT = 32
NCOL = 2048
NA = 128
BCELL = 64
CC = 384


def draw_ray_bins(key, part):
    first_key, second_key = jax.random.split(jax.random.fold_in(key, 17))
    col_sector = (jnp.arange(NCOL, dtype=jnp.int32) // COLS_DEV)[:, None]
    steps = jax.random.randint(first_key, (NCOL, DB), -1, 2).astype(jnp.int32)
    slots = jax.random.randint(second_key, (NCOL, DB), 0, BA).astype(jnp.int32)
    cycles = (jnp.arange(DB, dtype=jnp.int32) * BR // DB)[None, :]
    sectors = (col_sector + steps) % NSECT
    return (sectors * (BR * BA) + cycles * BA + slots).astype(jnp.int32)


def plant(values, key, low, high):
    place = [jax.random.randint(jax.random.fold_in(key, axis), (), 0, length) for axis, length in enumerate(values.shape)]
    main_axis = values.shape.index(max(values.shape))
    neighbour = place[:main_axis] + [(place[main_axis] + 1) % values.shape[main_axis]] + place[main_axis + 1:]
    return values.at[tuple(place)].set(low).at[tuple(neighbour)].set(high)


def levels(stream_key, shape, cuts, smallest, largest):
    factor_of, own = 1.0, jax.random.fold_in(stream_key, 6)
    for axis_at, blocks in cuts:
        draws = jnp.exp(jax.random.uniform(jax.random.fold_in(own, axis_at), (blocks,), jnp.float32, smallest / len(cuts), largest / len(cuts)))
        factor_of = factor_of * jnp.repeat(draws, shape[axis_at] // blocks).reshape([-1 if axis == axis_at else 1 for axis in range(len(shape))])
    return factor_of


def gaussian(own_key, shape, scale, reach, pieces=(), held_as=jnp.bfloat16):
    array = scale * jax.random.normal(own_key, shape, jnp.float32)
    if pieces:
        array = array * levels(own_key, shape, pieces, -0.22, 0.18)
    return jnp.clip(array, -reach, reach).astype(held_as)


def setup_inputs(seed: int = 0) -> dict:
    key_of = jax.random.split(jax.random.key(seed), 10)
    return {
        "image_feats": gaussian(key_of[0], (ROWS, NCOL, C), 1.0, 6.0, ((1, 32),)),
        "cam_weights": gaussian(key_of[1], (LAYERS, 9, C, C), (9 * C // 2) ** -0.5, 0.1875),
        "depth_weight": gaussian(key_of[2], (C, DB), (C // 16) ** -0.5, 1.5),
        "ray_bins": draw_ray_bins(jax.random.fold_in(key_of[9], 71), 0),
        "pillar_sums": gaussian(key_of[4], (2 * BR, 2 * NA, CL), 2.0, 12.0, ((1, 32),)),
        "pillar_counts": plant(jax.random.randint(key_of[5], (2 * BR, 2 * NA), 0, 9), jax.random.fold_in(key_of[5], 1), 0, 8).astype(jnp.int32),
        "lidar_weight": gaussian(key_of[6], (4, CL, CL), (2 * CL) ** -0.5, 0.375),
        "merge_weight": gaussian(key_of[7], (9, CC, CF), (9 * CC // 2) ** -0.5, 0.15625),
        "out_cotangent": gaussian(key_of[8], (BR, NA, CF), 1.0, 6.0, ((1, 32),)),
    }


def wrap_columns(values):
    return jnp.concatenate([values[:, -1:], values, values[:, :1]], axis=1)


def pad_rows(values):
    return jnp.pad(values, ((1, 1), (0, 0), (0, 0)))


def conv_taps(padded, weights, row_count, col_count):
    result = None
    for tap_index in range(9):
        down_step = tap_index // 3
        right_step = tap_index % 3
        window = padded[down_step:down_step + row_count, right_step:right_step + col_count]
        partial_value = jnp.dot(window.reshape(row_count * col_count, -1), weights[tap_index], preferred_element_type=jnp.float32)
        result = partial_value if result is None else result + partial_value
    return result.reshape(row_count, col_count, -1)


def conv_back(padded, weights, row_count, col_count):
    result = None
    for tap_index in range(9):
        down_step = tap_index // 3
        right_step = tap_index % 3
        window = padded[2 - down_step:2 - down_step + row_count, 2 - right_step:2 - right_step + col_count]
        partial_value = lax.dot_general(window.reshape(row_count * col_count, -1), weights[tap_index], (((1,), (1,)), ((), ())), preferred_element_type=jnp.float32)
        result = partial_value if result is None else result + partial_value
    return result.reshape(row_count, col_count, -1)


def depth_part(block, depth_weight):
    logits = jnp.einsum("hjc,ck->hjk", block.astype(jnp.float32), depth_weight.astype(jnp.float32))
    softened = jax.nn.softplus(logits) + 0.05
    totals = jnp.sum(softened, axis=2, keepdims=True)
    depth_probs = softened / totals
    probs_low = depth_probs.astype(jnp.bfloat16)
    return logits, totals, depth_probs, probs_low


def reference(image_feats, cam_weights, depth_weight, ray_bins, pillar_sums, pillar_counts, lidar_weight, merge_weight, out_cotangent):
    features = image_feats
    for layer_idx in range(LAYERS):
        conv_out = conv_taps(pad_rows(wrap_columns(features)), cam_weights[layer_idx], ROWS, NCOL)
        features = jax.nn.relu(conv_out).astype(jnp.bfloat16)

    def lift_block(grid, sector):
        begin_col = (sector * COLS_DEV).astype(jnp.int32)
        block = lax.dynamic_slice_in_dim(features, begin_col, COLS_DEV, 1)
        bins = lax.dynamic_slice_in_dim(ray_bins, begin_col, COLS_DEV, 0).reshape(-1)
        logits, totals, depth_probs, probs_low = depth_part(block, depth_weight)
        lifted = jnp.einsum("hjk,hjc->jkc", probs_low.astype(jnp.float32), block.astype(jnp.float32))
        grid = grid + jax.ops.segment_sum(lifted.reshape(-1, C), bins, num_segments=NSECT * BCELL)
        return grid, None

    grid, _ = lax.scan(lift_block, jnp.zeros((NSECT * BCELL, C), jnp.float32), jnp.arange(NSECT, dtype=jnp.int32))
    cam_bev = grid.reshape(NSECT, BR, BA, C).transpose(1, 0, 2, 3).reshape(BR, NA, C).astype(jnp.bfloat16)

    occupied = (pillar_counts > 0).astype(jnp.float32)
    divisor = jnp.maximum(pillar_counts, 1).astype(jnp.float32)
    pillar_feat = (pillar_sums.astype(jnp.float32) * (occupied / divisor)[:, :, None]).astype(jnp.bfloat16)
    grouped = pillar_feat.reshape(BR, 2, NA, 2, CL)
    lidar_sum = None
    for offset in range(4):
        window = grouped[:, offset // 2, :, offset % 2, :].reshape(BR * NA, CL)
        partial_value = jnp.dot(window, lidar_weight[offset], preferred_element_type=jnp.float32)
        lidar_sum = partial_value if lidar_sum is None else lidar_sum + partial_value
    lid_bev = jax.nn.relu(lidar_sum).reshape(BR, NA, CL).astype(jnp.bfloat16)

    merged_in = jnp.concatenate([cam_bev, lid_bev], axis=2)
    pre_act = conv_taps(pad_rows(wrap_columns(merged_in)), merge_weight, BR, NA)
    merged = jax.nn.silu(pre_act).astype(jnp.bfloat16)
    gating = jax.nn.sigmoid(pre_act)
    slopes = gating * (1.0 + pre_act * (1.0 - gating))
    grad_pre = (out_cotangent.astype(jnp.float32) * slopes).astype(jnp.bfloat16)
    grad_in = conv_back(pad_rows(wrap_columns(grad_pre)), merge_weight, BR, NA)
    lid_grad = grad_in[:, :, C:].astype(jnp.bfloat16)
    cam_bev_grad = grad_in[:, :, :C].astype(jnp.bfloat16)
    grad_table = cam_bev_grad.reshape(BR, NSECT, BA, C).transpose(1, 0, 2, 3).reshape(NSECT * BCELL, C)

    def back_block(sector):
        begin_col = (sector * COLS_DEV).astype(jnp.int32)
        block = lax.dynamic_slice_in_dim(features, begin_col, COLS_DEV, 1)
        bins = lax.dynamic_slice_in_dim(ray_bins, begin_col, COLS_DEV, 0).reshape(-1)
        logits, totals, depth_probs, probs_low = depth_part(block, depth_weight)
        grad_lift = jnp.take(grad_table, bins, axis=0).reshape(COLS_DEV, DB, C)
        grad_probs = jnp.einsum("jkc,hjc->hjk", grad_lift.astype(jnp.float32), block.astype(jnp.float32))
        grad_direct = jnp.einsum("hjk,jkc->hjc", probs_low.astype(jnp.float32), grad_lift.astype(jnp.float32))
        grad_soft = (grad_probs - jnp.sum(grad_probs * depth_probs, axis=2, keepdims=True)) / totals
        grad_logits = (grad_soft * jax.nn.sigmoid(logits)).astype(jnp.bfloat16)
        grad_depth = jnp.einsum("hjk,ck->hjc", grad_logits.astype(jnp.float32), depth_weight.astype(jnp.float32))
        return (grad_direct + grad_depth).astype(jnp.bfloat16)

    blocks = lax.map(back_block, jnp.arange(NSECT, dtype=jnp.int32))
    cam_grad = blocks.transpose(1, 0, 2, 3).reshape(ROWS, NCOL, C)
    return merged, cam_grad, lid_grad
```

```python
import functools

import jax
import jax.numpy as jnp
from jax import lax
from jax.experimental import pallas as pl
from jax.experimental.pallas import tpu as pltpu
from jax.sharding import PartitionSpec as P

AXES = ("branch", "strip")
CH = 8
BLOCK = 16


def rolled_sum(low, mid, high, period):
    rows = mid.shape[0]
    place = lax.broadcasted_iota(jnp.int32, mid.shape, 0) & (period - 1)
    down = jnp.where(place == 0, 0.0, pltpu.roll(low, 1, 0))
    up = jnp.where(place == period - 1, 0.0, pltpu.roll(high, rows - 1, 0))
    return mid + down + up


def conv_rows(src, pieces, weights, layer, height):
    taps = [
        jnp.concatenate([src[pl.ds(s + i * height, rows), :] for s, rows in pieces], axis=0)
        for i in range(3)
    ]
    x = jnp.concatenate(taps, axis=1)
    channels = taps[0].shape[1]
    z = [
        jnp.dot(
            x,
            weights[layer, 3 * dy : 3 * dy + 3].reshape(3 * channels, -1),
            preferred_element_type=jnp.float32,
        )
        for dy in range(3)
    ]
    total = rolled_sum(z[0], z[1], z[2], height)
    return jnp.maximum(total, 0.0).astype(jnp.bfloat16)


def one_hot_rows(rows, sources, source_of):
    p = lax.broadcasted_iota(jnp.int32, (rows, sources), 0)
    q = lax.broadcasted_iota(jnp.int32, (rows, sources), 1)
    return jnp.where(source_of(p) == q, 1.0, 0.0).astype(jnp.bfloat16)


def row_numbers(shape):
    return lax.broadcasted_iota(jnp.int32, shape, 0).astype(jnp.float32).astype(jnp.bfloat16)


def pick_of(row_id, codes, j):
    groups, lanes = row_id.shape
    code = jnp.broadcast_to(codes[pl.ds(j, 1), :], (16, lanes)).astype(jnp.bfloat16)
    code = jnp.concatenate([code] * (groups // 16), axis=0)
    one, zero = jnp.ones((), jnp.bfloat16), jnp.zeros((), jnp.bfloat16)
    return jnp.where(row_id[...] == code, one, zero)


def block_turn():
    shift = BLOCK.bit_length() - 1
    return one_hot_rows(
        BLOCK * BLOCK,
        BLOCK * BLOCK,
        lambda p: ((p & (BLOCK - 1)) << shift) + (p >> shift),
    )


def kernel(
    n, strips, cols, height, br, ba, bins_n,
    img_hbm, cw_hbm, wd_hbm, bins_hbm, pillars_hbm, counts_hbm, lw_hbm, cot_hbm, mw_hbm,
    merged_o, lidgrad_o, table, codes, feats, amat, probs, slope,
    img, cw, mw, xin, y1, y2, wd, bins, pillars, counts, lw, cot,
    wdp, sums, low, row_id, parts, sendbuf,
    rp1, rp2, rp3, rm1, rm2, rm3, win, lidwin, cotwin,
    local_sem, send_sem, recv_sem,
):
    me = lax.axis_index(AXES[0]) * strips + lax.axis_index(AXES[1])
    ch_rows = CH * height
    lanes = wdp.shape[0]

    def dev(d):
        t = lax.rem(me + d + n, n)
        return (t // strips, t % strips)

    barrier = pltpu.get_barrier_semaphore()
    for d in (1, 2, 3, -1, -2, -3):
        pl.semaphore_signal(
            barrier, inc=1, device_id=dev(d), device_id_type=pl.DeviceIdType.MESH
        )
    layers = cw.shape[0]
    small = [
        pltpu.make_async_copy(src, dst, local_sem.at[layers + 2 + i])
        for i, (src, dst) in enumerate(
            (
                (pillars_hbm, pillars), (counts_hbm, counts), (lw_hbm, lw), (cot_hbm, cot),
                (wd_hbm, wd), (bins_hbm, bins),
            )
        )
    ]
    for copy in small:
        copy.start()
    image = pltpu.make_async_copy(img_hbm, img, local_sem.at[layers + 1])
    image.start()
    fetches = [
        pltpu.make_async_copy(cw_hbm.at[k], cw.at[k], local_sem.at[k]) for k in range(layers)
    ]
    fetches.append(pltpu.make_async_copy(mw_hbm, mw, local_sem.at[layers]))
    for copy in fetches:
        copy.start()

    row_id[...] = row_numbers(row_id.shape)
    wdp[...] = jnp.zeros_like(wdp)
    codes[...] = jnp.full(codes.shape, -1.0, jnp.float32)
    parts[...] = jnp.zeros_like(parts)
    win[...] = jnp.zeros_like(win)
    for copy in small:
        copy.wait()
    sec = ba * br
    cot_own, lid_own = (ba + 1) * br, (ba + 2) * br
    cot_f = cot[...].astype(jnp.float32)
    for a in range(ba):
        cotwin[pl.ds(cot_own + a * br, br), :] = cot_f[:, a, :].astype(jnp.bfloat16)
    points = counts[...]
    scale = (points > 0).astype(jnp.float32) / jnp.maximum(points, 1).astype(jnp.float32)
    pil = pillars[...].astype(jnp.float32)
    pil = jnp.concatenate(
        [pil[k] * scale[:, k : k + 1] for k in range(2 * br)], axis=0
    ).astype(jnp.bfloat16)
    lb, la = br.bit_length() - 1, ba.bit_length() - 1

    def pillar_row(p):
        r, a, uv = p & (br - 1), (p >> lb) & (ba - 1), p >> (lb + la)
        return ((2 * r + (uv >> 1)) << (la + 1)) + 2 * a + (uv & 1)

    gathered = jnp.dot(
        one_hot_rows(4 * sec, 4 * sec, pillar_row), pil, preferred_element_type=jnp.float32
    ).astype(jnp.bfloat16)
    taps = jnp.concatenate([gathered[k * sec : (k + 1) * sec] for k in range(4)], axis=1)
    lid = jnp.dot(
        taps, lw[...].reshape(taps.shape[1], -1), preferred_element_type=jnp.float32
    )
    lidwin[pl.ds(lid_own, sec), :] = jnp.maximum(lid, 0.0).astype(jnp.bfloat16)

    cell = br * ba
    sh_cell, sh_ba, sh_br = cell.bit_length() - 1, ba.bit_length() - 1, br.bit_length() - 1
    raw = bins[...]
    off = (raw >> sh_cell) - me + 1
    off = jnp.where(off < 0, off + n, off)
    off = jnp.where(off >= n, off - n, off)
    in_cell = raw & (cell - 1)
    code = (((off << sh_ba) + (in_cell & (ba - 1))) << sh_br) + (in_cell >> sh_ba)
    codes[:, 0:bins_n] = code.astype(jnp.float32)
    wdp[0:bins_n, :] = wd[...]
    image.wait()
    turn = block_turn()
    for j0 in range(0, cols, BLOCK):
        for h0 in range(0, height, BLOCK):
            block = img[h0 : h0 + BLOCK, j0 : j0 + BLOCK, :].reshape(BLOCK * BLOCK, -1)
            turned = jnp.dot(turn, block, preferred_element_type=jnp.float32)
            turned = turned.astype(jnp.bfloat16)
            for c in range(BLOCK):
                at = (3 + j0 + c) * height + h0
                xin[pl.ds(at, BLOCK), :] = turned[c * BLOCK : (c + 1) * BLOCK]
    fetches[0].wait()

    def interior(src, dst, layer, first, shift, count, wide):
        def step(i, carry):
            c = jnp.minimum(first + wide * i, cols - first - wide) + shift
            at = pl.multiple_of(c * height, height)
            size = wide * height
            dst[pl.ds(at, size), :] = conv_rows(src, [(at, size)], cw, layer, height)
            return carry

        lax.fori_loop(0, count, step, 0)

    full = cols // CH
    interior(xin, y1, 0, 1, 2, full // 2, 2 * CH)
    pl.semaphore_wait(barrier, 6)

    messages = []

    def send(src, dst, d):
        m = len(messages)
        copy = pltpu.make_async_remote_copy(
            src_ref=src,
            dst_ref=dst,
            send_sem=send_sem.at[m],
            recv_sem=recv_sem.at[m],
            device_id=dev(d),
            device_id_type=pl.DeviceIdType.MESH,
        )
        copy.start()
        messages.append(copy)

    h3 = 3 * height
    send(xin.at[pl.ds(cols * height, h3)], xin.at[pl.ds(0, h3)], 1)
    send(xin.at[pl.ds(h3, h3)], xin.at[pl.ds((cols + 3) * height, h3)], -1)
    for window, start, edge in ((cotwin, cot_own, br), (lidwin, lid_own, 2 * br)):
        mine = window.at[pl.ds(start, sec)]
        send(mine, window.at[pl.ds(edge, sec)], 1)
        send(mine, window.at[pl.ds(start + sec, sec)], -1)
        last = window.at[pl.ds(start + sec - edge, edge)]
        send(last, window.at[pl.ds(0, edge)], 2)
        send(window.at[pl.ds(start, edge)], window.at[pl.ds(start + 2 * sec, edge)], -2)

    fetches[1].wait()
    interior(y1, y2, 1, 2, 1, full // 2, 2 * CH)
    fetches[2].wait()
    interior(y2, feats, 2, 3, 0, full // 2 - 1, 2 * CH)

    messages[0].wait_recv()
    messages[1].wait_recv()
    for layer, (src, dst, extra, done) in enumerate(
        ((xin, y1, 4, cols - 2), (y1, y2, 2, cols - 4), (y2, feats, 0, cols - 2 * CH))
    ):
        right = (3 + done) * height
        size = (cols + extra) * height - right
        edge = conv_rows(src, [(0, h3), (right, size)], cw, layer, height)
        dst[pl.ds(0, h3), :] = edge[:h3]
        dst[pl.ds(right, size), :] = edge[h3:]

    used = 3 * ba * br
    lane = lax.broadcasted_iota(jnp.int32, (ch_rows, lanes), 1)

    def soften(i, carry):
        at = pl.multiple_of(i * ch_rows, ch_rows)
        f = feats[pl.ds(at, ch_rows), :]
        logits = lax.dot_general(
            f, wdp[...], (((1,), (1,)), ((), ())), preferred_element_type=jnp.float32
        )
        e = jnp.exp(-jnp.abs(logits))
        soft = jnp.maximum(logits, 0.0) + jnp.log1p(e) + 0.05
        soft = jnp.where(lane < bins_n, soft, 0.0)
        inv = 1.0 / jnp.sum(soft, axis=1, keepdims=True)
        p = soft * inv
        probs[pl.ds(at, ch_rows), :] = p
        slope[pl.ds(at, ch_rows), :] = logits
        sums[pl.ds(at, ch_rows), :] = inv
        low[pl.ds(at, ch_rows), :] = p.astype(jnp.bfloat16)
        return carry

    lax.fori_loop(0, cols // CH, soften, 0)

    def lift(i, carry):
        for c in range(CH):
            j = i * CH + c
            at = pl.multiple_of(j * height, height)
            a = lax.dot_general(
                low[pl.ds(at, height), :],
                pick_of(row_id, codes, j),
                (((1,), (1,)), ((), ())),
                preferred_element_type=jnp.float32,
            )
            amat[pl.ds(at, height), :] = a.astype(jnp.bfloat16)
        return carry

    lax.fori_loop(0, cols // CH, lift, 0)

    def gather(i, carry):
        at = pl.multiple_of(i * 2 * ch_rows, 2 * ch_rows)
        parts[...] += lax.dot_general(
            amat[pl.ds(at, 2 * ch_rows), :],
            feats[pl.ds(at, 2 * ch_rows), :],
            (((0,), (0,)), ((), ())),
            preferred_element_type=jnp.float32,
        )
        return carry

    lax.fori_loop(0, cols // (2 * CH), gather, 0)

    mine = parts[0:used, :]
    sendbuf[...] = mine.astype(jnp.bfloat16)
    n1, n2, n3 = (2 * ba + 2) * br, (ba + 2) * br, 2 * br
    send(sendbuf.at[pl.ds(used - n1, n1)], rp1, 1)
    send(sendbuf.at[pl.ds(0, n1)], rm1, -1)
    send(sendbuf.at[pl.ds(used - n2, n2)], rp2, 2)
    send(sendbuf.at[pl.ds(0, n2)], rm2, -2)
    send(sendbuf.at[pl.ds(used - n3, n3)], rp3, 3)
    send(sendbuf.at[pl.ds(0, n3)], rm3, -3)

    def bend(i, carry):
        at = pl.multiple_of(i * ch_rows, ch_rows)
        sig = jax.nn.sigmoid(slope[pl.ds(at, ch_rows), :]) * sums[pl.ds(at, ch_rows), :]
        slope[pl.ds(at, ch_rows), :] = jnp.where(lane < bins_n, sig, 0.0)
        return carry

    lax.fori_loop(0, cols // CH, bend, 0)
    for copy in messages[2:10]:
        copy.wait_recv()
    fetches[layers].wait()
    channels = feats.shape[1]
    total = win.shape[0]
    act_rows = total - 2 * br

    def merge(source, lo, hi):
        x = jnp.concatenate([source[i * br : i * br + act_rows] for i in range(3)], axis=1)
        z = [
            jnp.dot(
                x,
                mw[3 * dy : 3 * dy + 3, lo:hi, :].reshape(3 * (hi - lo), -1),
                preferred_element_type=jnp.float32,
            )
            for dy in range(3)
        ]
        return rolled_sum(z[0], z[1], z[2], br)

    lid_act = merge(lidwin[...], channels, mw.shape[1])
    win[pl.ds(2 * br, used), :] = mine
    for copy in messages[10:]:
        copy.wait_recv()
    for got, size in ((rp1, n1), (rp2, n2), (rp3, n3)):
        win[pl.ds(0, size), :] += got[...].astype(jnp.float32)
    for got, size in ((rm1, n1), (rm2, n2), (rm3, n3)):
        win[pl.ds(total - size, size), :] += got[...].astype(jnp.float32)

    act = lid_act + merge(win[...].astype(jnp.bfloat16), 0, channels)
    gate = 1.0 / (1.0 + jnp.exp(-act))
    merged = (act * gate)[cot_own : cot_own + sec]
    merged_o[...] = jnp.stack(
        [merged[a * br : (a + 1) * br] for a in range(ba)], axis=1
    ).astype(jnp.bfloat16)
    grad_pre = (
        cotwin[...].astype(jnp.float32) * (gate * (1.0 + act * (1.0 - gate)))
    ).astype(jnp.bfloat16)

    def merge_back(first, rows, lo, hi):
        y = []
        for dy in range(3):
            acc = None
            for i in range(3):
                term = lax.dot_general(
                    grad_pre[first + (2 - i) * br : first + (2 - i) * br + rows],
                    mw[3 * dy + i, lo:hi, :],
                    (((1,), (1,)), ((), ())),
                    preferred_element_type=jnp.float32,
                )
                acc = term if acc is None else acc + term
            y.append(acc)
        return rolled_sum(y[2], y[1], y[0], br)

    table[...] = merge_back(0, used, 0, channels).astype(jnp.bfloat16)
    lid_grad = merge_back(sec, sec, channels, mw.shape[1])
    lidgrad_o[...] = jnp.stack(
        [lid_grad[a * br : (a + 1) * br] for a in range(ba)], axis=1
    ).astype(jnp.bfloat16)
    for copy in messages:
        copy.wait_send()


def back_kernel(
    height, bins_n, steps,
    feats, amat, probs, slope, codes, table, wd, merged, lid_grad,
    camgrad_o, merged_o, lidgrad_o,
    wdp, row_id, buf, sem,
):
    ch_rows = CH * height
    small = [
        pltpu.make_async_copy(merged, merged_o, sem.at[2]),
        pltpu.make_async_copy(lid_grad, lidgrad_o, sem.at[3]),
    ]
    for copy in small:
        copy.start()
    wdp[...] = jnp.zeros_like(wdp)
    wdp[0:bins_n, :] = wd[...]
    row_id[...] = row_numbers(row_id.shape)
    turn = block_turn()
    chunks = BLOCK // CH

    def out_copy(step, slot):
        return pltpu.make_async_copy(
            buf.at[slot],
            camgrad_o.at[:, pl.ds(pl.multiple_of(step * BLOCK, BLOCK), BLOCK), :],
            sem.at[slot],
        )

    def body(step, carry):
        slot = step & 1

        @pl.when(step >= 2)
        def _():
            out_copy(step - 2, slot).wait()

        tab = table[...]
        blocks = []
        for k in range(chunks):
            at = pl.multiple_of((step * chunks + k) * ch_rows, ch_rows)
            rows = pl.ds(at, ch_rows)
            g = lax.dot_general(
                feats[rows, :], tab, (((1,), (1,)), ((), ())), preferred_element_type=jnp.float32
            ).astype(jnp.bfloat16)
            direct = jnp.dot(amat[rows, :], tab, preferred_element_type=jnp.float32)
            gp = jnp.concatenate(
                [
                    jnp.dot(
                        g[c * height : (c + 1) * height],
                        pick_of(row_id, codes, (step * chunks + k) * CH + c),
                        preferred_element_type=jnp.float32,
                    )
                    for c in range(CH)
                ],
                axis=0,
            )
            mean = jnp.sum(gp * probs[rows, :], axis=1, keepdims=True)
            gl = ((gp - mean) * slope[rows, :]).astype(jnp.bfloat16)
            depth = jnp.dot(gl, wdp[...], preferred_element_type=jnp.float32)
            blocks.append((direct + depth).astype(jnp.bfloat16))
        block = jnp.concatenate(blocks, axis=0)
        for h0 in range(0, height, BLOCK):
            part = jnp.concatenate(
                [block[c * height + h0 : c * height + h0 + BLOCK] for c in range(BLOCK)], axis=0
            )
            turned = jnp.dot(turn, part, preferred_element_type=jnp.float32)
            buf[slot, h0 : h0 + BLOCK, :, :] = turned.astype(jnp.bfloat16).reshape(
                BLOCK, BLOCK, -1
            )
        out_copy(step, slot).start()
        return carry

    lax.fori_loop(0, steps, body, 0)
    for k in (2, 1):
        out_copy(steps - k, (steps - k) & 1).wait()
    for copy in small:
        copy.wait()


def local(
    n, strips,
    image_feats, cam_weights, depth_weight, ray_bins, pillar_sums, pillar_counts,
    lidar_weight, merge_weight, out_cotangent,
):
    height, cols, channels = image_feats.shape
    br, ba, cf = out_cotangent.shape
    bins_n = depth_weight.shape[1]
    cl = pillar_sums.shape[2]
    lanes = -(-bins_n // 128) * 128
    used = groups = 3 * ba * br
    total = (3 * ba + 4) * br
    bf, f32 = jnp.bfloat16, jnp.float32

    vm = pl.BlockSpec(memory_space=pltpu.VMEM)
    hbm = pl.BlockSpec(memory_space=pltpu.HBM)
    n1, n2, n3 = (2 * ba + 2) * br, (ba + 2) * br, 2 * br
    rows = cols * height
    turned_counts = pillar_counts.T
    turned_depth = depth_weight.T
    merged, lid_grad, table, codes, feats, amat, probs, slope = pl.pallas_call(
        functools.partial(kernel, n, strips, cols, height, br, ba, bins_n),
        out_shape=(
            pltpu.VMEM((br, ba, cf), bf),
            pltpu.VMEM((br, ba, cl), bf),
            pltpu.VMEM((groups, channels), bf),
            pltpu.VMEM((cols, lanes), f32),
            pltpu.VMEM((rows, channels), bf),
            pltpu.VMEM((rows, groups), bf),
            pltpu.VMEM((rows, lanes), f32),
            pltpu.VMEM((rows, lanes), f32),
        ),
        in_specs=[hbm] * 9,
        out_specs=(vm,) * 8,
        scratch_shapes=[
            pltpu.VMEM(image_feats.shape, bf),
            pltpu.VMEM(cam_weights.shape, bf),
            pltpu.VMEM(merge_weight.shape, bf),
            pltpu.VMEM(((cols + 6) * height, channels), bf),
            pltpu.VMEM(((cols + 4) * height, channels), bf),
            pltpu.VMEM(((cols + 2) * height, channels), bf),
            pltpu.VMEM(turned_depth.shape, bf),
            pltpu.VMEM(ray_bins.shape, jnp.int32),
            pltpu.VMEM(pillar_sums.shape, bf),
            pltpu.VMEM(turned_counts.shape, jnp.int32),
            pltpu.VMEM(lidar_weight.shape, bf),
            pltpu.VMEM(out_cotangent.shape, bf),
            pltpu.VMEM((lanes, channels), bf),
            pltpu.VMEM((cols * height, 1), f32),
            pltpu.VMEM((cols * height, lanes), bf),
            pltpu.VMEM((groups, lanes), bf),
            pltpu.VMEM((groups, channels), f32),
            pltpu.VMEM((used, channels), bf),
            pltpu.VMEM((n1, channels), bf),
            pltpu.VMEM((n2, channels), bf),
            pltpu.VMEM((n3, channels), bf),
            pltpu.VMEM((n1, channels), bf),
            pltpu.VMEM((n2, channels), bf),
            pltpu.VMEM((n3, channels), bf),
            pltpu.VMEM((total, channels), f32),
            pltpu.VMEM((total, cl), bf),
            pltpu.VMEM((total - 2 * br, cf), bf),
            pltpu.SemaphoreType.DMA((cam_weights.shape[0] + 8,)),
            pltpu.SemaphoreType.DMA((16,)),
            pltpu.SemaphoreType.DMA((16,)),
        ],
        compiler_params=pltpu.CompilerParams(
            collective_id=0, has_side_effects=True, vmem_limit_bytes=40 * 1024 * 1024
        ),
        name="bev",
    )(
        *(
            pltpu.with_memory_space_constraint(x, pltpu.HBM)
            for x in (
                image_feats, cam_weights, turned_depth, ray_bins, pillar_sums, turned_counts,
                lidar_weight, out_cotangent, merge_weight,
            )
        )
    )
    steps = cols // BLOCK
    cam_grad, merged, lid_grad = pl.pallas_call(
        functools.partial(back_kernel, height, bins_n, steps),
        out_shape=(
            pltpu.HBM((height, cols, channels), bf),
            pltpu.HBM((br, ba, cf), bf),
            pltpu.HBM((br, ba, cl), bf),
        ),
        in_specs=[vm] * 9,
        out_specs=(hbm,) * 3,
        scratch_shapes=[
            pltpu.VMEM((lanes, channels), bf),
            pltpu.VMEM((groups, lanes), bf),
            pltpu.VMEM((2, height, BLOCK, channels), bf),
            pltpu.SemaphoreType.DMA((4,)),
        ],
        compiler_params=pltpu.CompilerParams(vmem_limit_bytes=40 * 1024 * 1024),
        name="back",
    )(feats, amat, probs, slope, codes, table, turned_depth, merged, lid_grad)
    return merged, cam_grad, lid_grad


def solution(mesh):
    strips = mesh.shape["strip"]
    n = mesh.shape["branch"] * strips
    placed = (
        P(None, AXES, None),
        P(),
        P(),
        P(AXES, None),
        P(None, AXES, None),
        P(None, AXES),
        P(),
        P(),
        P(None, AXES, None),
    )
    return jax.shard_map(
        functools.partial(local, n, strips),
        mesh=mesh,
        in_specs=placed,
        out_specs=(P(None, AXES, None),) * 3,
        check_vma=False,
    )
```

```python
import functools

import jax
import jax.numpy as jnp
from jax import lax
from jax.experimental import pallas as pl
from jax.experimental.pallas import tpu as pltpu
from jax.sharding import PartitionSpec as P

AXES = ("branch", "strip")
CH = 8
BLOCK = 16


def rolled_sum(low, mid, high, period):
    rows = mid.shape[0]
    place = lax.broadcasted_iota(jnp.int32, mid.shape, 0) & (period - 1)
    down = jnp.where(place == 0, 0.0, pltpu.roll(low, 1, 0))
    up = jnp.where(place == period - 1, 0.0, pltpu.roll(high, rows - 1, 0))
    return mid + down + up


def conv_rows(src, pieces, weights, layer, height):
    taps = [
        jnp.concatenate([src[pl.ds(s + i * height, rows), :] for s, rows in pieces], axis=0)
        for i in range(3)
    ]
    x = jnp.concatenate(taps, axis=1)
    channels = taps[0].shape[1]
    z = [
        jnp.dot(
            x,
            weights[layer, 3 * dy : 3 * dy + 3].reshape(3 * channels, -1),
            preferred_element_type=jnp.float32,
        )
        for dy in range(3)
    ]
    total = rolled_sum(z[0], z[1], z[2], height)
    return jnp.maximum(total, 0.0).astype(jnp.bfloat16)


def one_hot_rows(rows, sources, source_of):
    p = lax.broadcasted_iota(jnp.int32, (rows, sources), 0)
    q = lax.broadcasted_iota(jnp.int32, (rows, sources), 1)
    return jnp.where(source_of(p) == q, 1.0, 0.0).astype(jnp.bfloat16)


def row_numbers(shape):
    return lax.broadcasted_iota(jnp.int32, shape, 0).astype(jnp.float32).astype(jnp.bfloat16)


def one_hot(hit):
    return jnp.where(hit, jnp.ones((), jnp.bfloat16), jnp.zeros((), jnp.bfloat16))


def pick_of(row_id, codes, j):
    groups, lanes = row_id.shape
    code = jnp.broadcast_to(codes[pl.ds(j, 1), :], (16, lanes)).astype(jnp.bfloat16)
    code = jnp.concatenate([code] * (groups // 16), axis=0)
    return one_hot(row_id[...] == code)


def block_turn():
    shift = BLOCK.bit_length() - 1
    return one_hot_rows(
        BLOCK * BLOCK,
        BLOCK * BLOCK,
        lambda p: ((p & (BLOCK - 1)) << shift) + (p >> shift),
    )


def kernel(
    n, strips, cols, height, br, ba, bins_n,
    img_hbm, cw_hbm, wd_hbm, bins_hbm, pillars_hbm, counts_hbm, lw_hbm, cot_hbm, mw_hbm,
    merged_o, lidgrad_o, table, picks, feats, amat, probs, slope,
    img, cw, mw, xin, y1, y2, wd, bins, pillars, counts, lw, cot,
    wdp, sums, low, row_id, codes, routes, sendbuf,
    rp1, rp2, rp3, rm1, rm2, rm3, win, lidwin, cotwin,
    local_sem, send_sem, recv_sem,
):
    me = lax.axis_index(AXES[0]) * strips + lax.axis_index(AXES[1])
    ch_rows = CH * height
    lanes = wdp.shape[0]

    def dev(d):
        t = lax.rem(me + d + n, n)
        return (t // strips, t % strips)

    barrier = pltpu.get_barrier_semaphore()
    for d in (1, 2, 3, -1, -2, -3):
        pl.semaphore_signal(
            barrier, inc=1, device_id=dev(d), device_id_type=pl.DeviceIdType.MESH
        )
    layers = cw.shape[0]
    small = [
        pltpu.make_async_copy(src, dst, local_sem.at[layers + 2 + i])
        for i, (src, dst) in enumerate(
            (
                (bins_hbm, bins), (pillars_hbm, pillars), (counts_hbm, counts), (lw_hbm, lw),
                (cot_hbm, cot), (wd_hbm, wd),
            )
        )
    ]
    for copy in small:
        copy.start()
    image = pltpu.make_async_copy(img_hbm, img, local_sem.at[layers + 1])
    image.start()
    fetches = [
        pltpu.make_async_copy(cw_hbm.at[k], cw.at[k], local_sem.at[k]) for k in range(layers)
    ]
    fetches.append(pltpu.make_async_copy(mw_hbm, mw, local_sem.at[layers]))
    for copy in fetches:
        copy.start()

    row_id[...] = row_numbers(row_id.shape)
    wdp[...] = jnp.zeros_like(wdp)
    codes[...] = jnp.full(codes.shape, -1.0, jnp.float32)
    win[...] = jnp.zeros_like(win)
    small[0].wait()
    cell = br * ba
    sh_cell, sh_ba, sh_br = cell.bit_length() - 1, ba.bit_length() - 1, br.bit_length() - 1
    raw = bins[...]
    off = (raw >> sh_cell) - me + 1
    off = jnp.where(off < 0, off + n, off)
    off = jnp.where(off >= n, off - n, off)
    in_cell = raw & (cell - 1)
    code = (((off << sh_ba) + (in_cell & (ba - 1))) << sh_br) + (in_cell >> sh_ba)
    codes[:, 0:bins_n] = code.astype(jnp.float32)
    turned_codes = jnp.transpose(codes[...])
    cells = lax.broadcasted_iota(jnp.int32, routes.shape[1:], 1)
    cells = cells.astype(jnp.float32).astype(jnp.bfloat16)
    for j in range(cols):
        code = jnp.broadcast_to(turned_codes[:, j : j + 1], cells.shape).astype(jnp.bfloat16)
        routes[j] = one_hot(code == cells)
    for copy in small[1:]:
        copy.wait()
    sec = ba * br
    cot_own, lid_own = (ba + 1) * br, (ba + 2) * br
    cot_f = cot[...].astype(jnp.float32)
    for a in range(ba):
        cotwin[pl.ds(cot_own + a * br, br), :] = cot_f[:, a, :].astype(jnp.bfloat16)
    points = counts[...]
    scale = (points > 0).astype(jnp.float32) / jnp.maximum(points, 1).astype(jnp.float32)
    pil = pillars[...].astype(jnp.float32)
    pil = jnp.concatenate(
        [pil[k] * scale[:, k : k + 1] for k in range(2 * br)], axis=0
    ).astype(jnp.bfloat16)
    lb, la = br.bit_length() - 1, ba.bit_length() - 1

    def pillar_row(p):
        r, a, uv = p & (br - 1), (p >> lb) & (ba - 1), p >> (lb + la)
        return ((2 * r + (uv >> 1)) << (la + 1)) + 2 * a + (uv & 1)

    gathered = jnp.dot(
        one_hot_rows(4 * sec, 4 * sec, pillar_row), pil, preferred_element_type=jnp.float32
    ).astype(jnp.bfloat16)
    taps = jnp.concatenate([gathered[k * sec : (k + 1) * sec] for k in range(4)], axis=1)
    lid = jnp.dot(
        taps, lw[...].reshape(taps.shape[1], -1), preferred_element_type=jnp.float32
    )
    lidwin[pl.ds(lid_own, sec), :] = jnp.maximum(lid, 0.0).astype(jnp.bfloat16)

    wdp[0:bins_n, :] = wd[...]
    image.wait()
    turn = block_turn()
    for j0 in range(0, cols, BLOCK):
        for h0 in range(0, height, BLOCK):
            block = img[h0 : h0 + BLOCK, j0 : j0 + BLOCK, :].reshape(BLOCK * BLOCK, -1)
            turned = jnp.dot(turn, block, preferred_element_type=jnp.float32)
            turned = turned.astype(jnp.bfloat16)
            for c in range(BLOCK):
                at = (3 + j0 + c) * height + h0
                xin[pl.ds(at, BLOCK), :] = turned[c * BLOCK : (c + 1) * BLOCK]
    fetches[0].wait()

    def interior(src, dst, layer, first, shift, count, wide):
        def step(i, carry):
            c = jnp.minimum(first + wide * i, cols - first - wide) + shift
            at = pl.multiple_of(c * height, height)
            size = wide * height
            dst[pl.ds(at, size), :] = conv_rows(src, [(at, size)], cw, layer, height)
            return carry

        lax.fori_loop(0, count, step, 0)

    full = cols // CH
    interior(xin, y1, 0, 1, 2, full // 2, 2 * CH)
    pl.semaphore_wait(barrier, 6)

    messages = []

    def send(src, dst, d):
        m = len(messages)
        copy = pltpu.make_async_remote_copy(
            src_ref=src,
            dst_ref=dst,
            send_sem=send_sem.at[m],
            recv_sem=recv_sem.at[m],
            device_id=dev(d),
            device_id_type=pl.DeviceIdType.MESH,
        )
        copy.start()
        messages.append(copy)

    h3 = 3 * height
    send(xin.at[pl.ds(cols * height, h3)], xin.at[pl.ds(0, h3)], 1)
    send(xin.at[pl.ds(h3, h3)], xin.at[pl.ds((cols + 3) * height, h3)], -1)
    for window, start, edge in ((cotwin, cot_own, br), (lidwin, lid_own, 2 * br)):
        mine = window.at[pl.ds(start, sec)]
        send(mine, window.at[pl.ds(edge, sec)], 1)
        send(mine, window.at[pl.ds(start + sec, sec)], -1)
        last = window.at[pl.ds(start + sec - edge, edge)]
        send(last, window.at[pl.ds(0, edge)], 2)
        send(window.at[pl.ds(start, edge)], window.at[pl.ds(start + 2 * sec, edge)], -2)

    fetches[1].wait()
    interior(y1, y2, 1, 2, 1, full // 2, 2 * CH)
    fetches[2].wait()
    interior(y2, feats, 2, 3, 0, full // 2 - 1, 2 * CH)

    messages[0].wait_recv()
    messages[1].wait_recv()
    for layer, (src, dst, extra, done) in enumerate(
        ((xin, y1, 4, cols - 2), (y1, y2, 2, cols - 4), (y2, feats, 0, cols - 2 * CH))
    ):
        right = (3 + done) * height
        size = (cols + extra) * height - right
        edge = conv_rows(src, [(0, h3), (right, size)], cw, layer, height)
        dst[pl.ds(0, h3), :] = edge[:h3]
        dst[pl.ds(right, size), :] = edge[h3:]

    used = 3 * ba * br
    wide = 2 * CH * height
    lane = lax.broadcasted_iota(jnp.int32, (wide, lanes), 1)
    for at in range(0, cols * height, wide):
        rows = pl.ds(at, wide)
        logits = lax.dot_general(
            feats[rows, :], wdp[...], (((1,), (1,)), ((), ())), preferred_element_type=jnp.float32
        )
        e = jnp.exp(-jnp.abs(logits))
        soft = jnp.maximum(logits, 0.0) + jnp.log(1.0 + e) + 0.05
        soft = jnp.where(lane < bins_n, soft, 0.0)
        inv = 1.0 / jnp.sum(soft, axis=1, keepdims=True)
        p = soft * inv
        probs[rows, :] = p
        slope[rows, :] = logits
        sums[rows, :] = inv
        low[rows, :] = p.astype(jnp.bfloat16)
    for j in range(cols):
        rows = pl.ds(j * height, height)
        a = jnp.dot(low[rows, :], routes[j], preferred_element_type=jnp.float32)
        amat[rows, :] = a.astype(jnp.bfloat16)
    mine = lax.dot_general(
        amat[...], feats[...], (((0,), (0,)), ((), ())), preferred_element_type=jnp.float32
    )
    sendbuf[...] = mine.astype(jnp.bfloat16)
    n1, n2, n3 = (2 * ba + 2) * br, (ba + 2) * br, 2 * br
    send(sendbuf.at[pl.ds(used - n1, n1)], rp1, 1)
    send(sendbuf.at[pl.ds(0, n1)], rm1, -1)
    send(sendbuf.at[pl.ds(used - n2, n2)], rp2, 2)
    send(sendbuf.at[pl.ds(0, n2)], rm2, -2)
    send(sendbuf.at[pl.ds(used - n3, n3)], rp3, 3)
    send(sendbuf.at[pl.ds(0, n3)], rm3, -3)

    for at in range(0, cols * height, wide):
        rows = pl.ds(at, wide)
        sig = jax.nn.sigmoid(slope[rows, :]) * sums[rows, :]
        slope[rows, :] = jnp.where(lane < bins_n, sig, 0.0)
    for j in range(0, cols, 2):
        picks[j // 2] = jnp.concatenate(
            [pick_of(row_id, codes, j), pick_of(row_id, codes, j + 1)], axis=1
        )
    for copy in messages[2:10]:
        copy.wait_recv()
    fetches[layers].wait()
    channels = feats.shape[1]
    total = win.shape[0]
    act_rows = total - 2 * br

    def merge(source, lo, hi):
        x = jnp.concatenate([source[i * br : i * br + act_rows] for i in range(3)], axis=1)
        z = [
            jnp.dot(
                x,
                mw[3 * dy : 3 * dy + 3, lo:hi, :].reshape(3 * (hi - lo), -1),
                preferred_element_type=jnp.float32,
            )
            for dy in range(3)
        ]
        return rolled_sum(z[0], z[1], z[2], br)

    lid_act = merge(lidwin[...], channels, mw.shape[1])
    win[pl.ds(2 * br, used), :] = mine
    for copy in messages[10:]:
        copy.wait_recv()
    for got, size in ((rp1, n1), (rp2, n2), (rp3, n3)):
        win[pl.ds(0, size), :] += got[...].astype(jnp.float32)
    for got, size in ((rm1, n1), (rm2, n2), (rm3, n3)):
        win[pl.ds(total - size, size), :] += got[...].astype(jnp.float32)

    act = lid_act + merge(win[...].astype(jnp.bfloat16), 0, channels)
    gate = 1.0 / (1.0 + jnp.exp(-act))
    merged = (act * gate)[cot_own : cot_own + sec]
    merged_o[...] = jnp.stack(
        [merged[a * br : (a + 1) * br] for a in range(ba)], axis=1
    ).astype(jnp.bfloat16)
    grad_pre = (
        cotwin[...].astype(jnp.float32) * (gate * (1.0 + act * (1.0 - gate)))
    ).astype(jnp.bfloat16)

    def merge_back(first, rows, lo, hi):
        y = []
        for dy in range(3):
            acc = None
            for i in range(3):
                term = lax.dot_general(
                    grad_pre[first + (2 - i) * br : first + (2 - i) * br + rows],
                    mw[3 * dy + i, lo:hi, :],
                    (((1,), (1,)), ((), ())),
                    preferred_element_type=jnp.float32,
                )
                acc = term if acc is None else acc + term
            y.append(acc)
        return rolled_sum(y[2], y[1], y[0], br)

    table[...] = merge_back(0, used, 0, channels).astype(jnp.bfloat16)
    lid_grad = merge_back(sec, sec, channels, mw.shape[1])
    lidgrad_o[...] = jnp.stack(
        [lid_grad[a * br : (a + 1) * br] for a in range(ba)], axis=1
    ).astype(jnp.bfloat16)
    for copy in messages:
        copy.wait_send()


def back_kernel(
    height, bins_n, steps,
    feats, amat, probs, slope, picks, table, wd, merged, lid_grad,
    camgrad_o, merged_o, lidgrad_o,
    wdp, buf, sem,
):
    lanes = wdp.shape[0]
    copies = [
        pltpu.make_async_copy(merged, merged_o, sem.at[steps]),
        pltpu.make_async_copy(lid_grad, lidgrad_o, sem.at[steps + 1]),
    ]
    for copy in copies:
        copy.start()
    wdp[...] = jnp.zeros_like(wdp)
    wdp[0:bins_n, :] = wd[...]
    turn = block_turn()
    tab = table[...]
    wide = BLOCK * height
    for step in range(steps):
        rows = pl.ds(step * wide, wide)
        g = lax.dot_general(
            feats[rows, :], tab, (((1,), (1,)), ((), ())), preferred_element_type=jnp.float32
        ).astype(jnp.bfloat16)
        direct = jnp.dot(amat[rows, :], tab, preferred_element_type=jnp.float32)
        gp = []
        for c in range(0, BLOCK, 2):
            both = jnp.dot(
                g[c * height : (c + 2) * height],
                picks[(step * BLOCK + c) // 2],
                preferred_element_type=jnp.float32,
            )
            gp.append(both[:height, :lanes])
            gp.append(both[height:, lanes:])
        gp = jnp.concatenate(gp, axis=0)
        mean = jnp.sum(gp * probs[rows, :], axis=1, keepdims=True)
        gl = ((gp - mean) * slope[rows, :]).astype(jnp.bfloat16)
        depth = jnp.dot(gl, wdp[...], preferred_element_type=jnp.float32)
        block = (direct + depth).astype(jnp.bfloat16)
        for h0 in range(0, height, BLOCK):
            part = jnp.concatenate(
                [block[c * height + h0 : c * height + h0 + BLOCK] for c in range(BLOCK)], axis=0
            )
            turned = jnp.dot(turn, part, preferred_element_type=jnp.float32)
            buf[h0 : h0 + BLOCK, pl.ds(step * BLOCK, BLOCK), :] = turned.astype(
                jnp.bfloat16
            ).reshape(BLOCK, BLOCK, -1)
        done = pl.ds(step * BLOCK, BLOCK)
        copy = pltpu.make_async_copy(buf.at[:, done, :], camgrad_o.at[:, done, :], sem.at[step])
        copy.start()
        copies.append(copy)
    for copy in copies:
        copy.wait()


def local(
    n, strips,
    image_feats, cam_weights, depth_weight, ray_bins, pillar_sums, pillar_counts,
    lidar_weight, merge_weight, out_cotangent,
):
    height, cols, channels = image_feats.shape
    br, ba, cf = out_cotangent.shape
    bins_n = depth_weight.shape[1]
    cl = pillar_sums.shape[2]
    lanes = -(-bins_n // 128) * 128
    used = groups = 3 * ba * br
    total = (3 * ba + 4) * br
    bf, f32 = jnp.bfloat16, jnp.float32

    vm = pl.BlockSpec(memory_space=pltpu.VMEM)
    hbm = pl.BlockSpec(memory_space=pltpu.HBM)
    n1, n2, n3 = (2 * ba + 2) * br, (ba + 2) * br, 2 * br
    rows = cols * height
    turned_counts = pillar_counts.T
    turned_depth = depth_weight.T
    merged, lid_grad, table, picks, feats, amat, probs, slope = pl.pallas_call(
        functools.partial(kernel, n, strips, cols, height, br, ba, bins_n),
        out_shape=(
            pltpu.VMEM((br, ba, cf), bf),
            pltpu.VMEM((br, ba, cl), bf),
            pltpu.VMEM((groups, channels), bf),
            pltpu.VMEM((cols // 2, groups, 2 * lanes), bf),
            pltpu.VMEM((rows, channels), bf),
            pltpu.VMEM((rows, groups), bf),
            pltpu.VMEM((rows, lanes), f32),
            pltpu.VMEM((rows, lanes), f32),
        ),
        in_specs=[hbm] * 9,
        out_specs=(vm,) * 8,
        scratch_shapes=[
            pltpu.VMEM(image_feats.shape, bf),
            pltpu.VMEM(cam_weights.shape, bf),
            pltpu.VMEM(merge_weight.shape, bf),
            pltpu.VMEM(((cols + 6) * height, channels), bf),
            pltpu.VMEM(((cols + 4) * height, channels), bf),
            pltpu.VMEM(((cols + 2) * height, channels), bf),
            pltpu.VMEM(turned_depth.shape, bf),
            pltpu.VMEM(ray_bins.shape, jnp.int32),
            pltpu.VMEM(pillar_sums.shape, bf),
            pltpu.VMEM(turned_counts.shape, jnp.int32),
            pltpu.VMEM(lidar_weight.shape, bf),
            pltpu.VMEM(out_cotangent.shape, bf),
            pltpu.VMEM((lanes, channels), bf),
            pltpu.VMEM((cols * height, 1), f32),
            pltpu.VMEM((cols * height, lanes), bf),
            pltpu.VMEM((groups, lanes), bf),
            pltpu.VMEM((cols, lanes), f32),
            pltpu.VMEM((cols, lanes, groups), bf),
            pltpu.VMEM((used, channels), bf),
            pltpu.VMEM((n1, channels), bf),
            pltpu.VMEM((n2, channels), bf),
            pltpu.VMEM((n3, channels), bf),
            pltpu.VMEM((n1, channels), bf),
            pltpu.VMEM((n2, channels), bf),
            pltpu.VMEM((n3, channels), bf),
            pltpu.VMEM((total, channels), f32),
            pltpu.VMEM((total, cl), bf),
            pltpu.VMEM((total - 2 * br, cf), bf),
            pltpu.SemaphoreType.DMA((cam_weights.shape[0] + 8,)),
            pltpu.SemaphoreType.DMA((16,)),
            pltpu.SemaphoreType.DMA((16,)),
        ],
        compiler_params=pltpu.CompilerParams(
            collective_id=0, has_side_effects=True, vmem_limit_bytes=44 * 1024 * 1024
        ),
        name="bev",
    )(
        *(
            pltpu.with_memory_space_constraint(x, pltpu.HBM)
            for x in (
                image_feats, cam_weights, turned_depth, ray_bins, pillar_sums, turned_counts,
                lidar_weight, out_cotangent, merge_weight,
            )
        )
    )
    steps = cols // BLOCK
    cam_grad, merged, lid_grad = pl.pallas_call(
        functools.partial(back_kernel, height, bins_n, steps),
        out_shape=(
            pltpu.HBM((height, cols, channels), bf),
            pltpu.HBM((br, ba, cf), bf),
            pltpu.HBM((br, ba, cl), bf),
        ),
        in_specs=[vm] * 9,
        out_specs=(hbm,) * 3,
        scratch_shapes=[
            pltpu.VMEM((lanes, channels), bf),
            pltpu.VMEM((height, cols, channels), bf),
            pltpu.SemaphoreType.DMA((steps + 2,)),
        ],
        compiler_params=pltpu.CompilerParams(vmem_limit_bytes=20 * 1024 * 1024),
        name="back",
    )(feats, amat, probs, slope, picks, table, turned_depth, merged, lid_grad)
    return merged, cam_grad, lid_grad


def solution(mesh):
    strips = mesh.shape["strip"]
    n = mesh.shape["branch"] * strips
    placed = (
        P(None, AXES, None),
        P(),
        P(),
        P(AXES, None),
        P(None, AXES, None),
        P(None, AXES),
        P(),
        P(),
        P(None, AXES, None),
    )
    return jax.shard_map(
        functools.partial(local, n, strips),
        mesh=mesh,
        in_specs=placed,
        out_specs=(P(None, AXES, None),) * 3,
        check_vma=False,
    )
```

```python
import functools

import jax
import jax.numpy as jnp
from jax import lax
from jax.experimental import pallas as pl
from jax.experimental.pallas import tpu as pltpu
from jax.sharding import PartitionSpec as P

AXES = ("branch", "strip")
CH = 8
BLOCK = 16


def rolled_sum(low, mid, high, period):
    rows = mid.shape[0]
    place = lax.broadcasted_iota(jnp.int32, mid.shape, 0) & (period - 1)
    down = jnp.where(place == 0, 0.0, pltpu.roll(low, 1, 0))
    up = jnp.where(place == period - 1, 0.0, pltpu.roll(high, rows - 1, 0))
    return mid + down + up


def conv_rows(src, pieces, weights, layer, height):
    taps = [
        jnp.concatenate([src[pl.ds(s + i * height, rows), :] for s, rows in pieces], axis=0)
        for i in range(3)
    ]
    x = jnp.concatenate(taps, axis=1)
    channels = taps[0].shape[1]
    z = [
        jnp.dot(
            x,
            weights[layer, 3 * dy : 3 * dy + 3].reshape(3 * channels, -1),
            preferred_element_type=jnp.float32,
        )
        for dy in range(3)
    ]
    total = rolled_sum(z[0], z[1], z[2], height)
    return jnp.maximum(total, 0.0).astype(jnp.bfloat16)


def one_hot_rows(rows, sources, source_of):
    p = lax.broadcasted_iota(jnp.int32, (rows, sources), 0)
    q = lax.broadcasted_iota(jnp.int32, (rows, sources), 1)
    return jnp.where(source_of(p) == q, 1.0, 0.0).astype(jnp.bfloat16)


def row_numbers(shape):
    return lax.broadcasted_iota(jnp.int32, shape, 0).astype(jnp.float32).astype(jnp.bfloat16)


def one_hot(hit):
    return jnp.where(hit, jnp.ones((), jnp.bfloat16), jnp.zeros((), jnp.bfloat16))


def pick_of(row_id, codes, j):
    groups, lanes = row_id.shape
    code = jnp.broadcast_to(codes[pl.ds(j, 1), :], (16, lanes)).astype(jnp.bfloat16)
    code = jnp.concatenate([code] * (groups // 16), axis=0)
    return one_hot(row_id[...] == code)


def block_turn():
    shift = BLOCK.bit_length() - 1
    return one_hot_rows(
        BLOCK * BLOCK,
        BLOCK * BLOCK,
        lambda p: ((p & (BLOCK - 1)) << shift) + (p >> shift),
    )


def kernel(
    n, strips, cols, height, br, ba, bins_n,
    img_hbm, cw_hbm, wd_hbm, bins_hbm, pillars_hbm, counts_hbm, lw_hbm, cot_hbm, mw_hbm,
    merged_o, lidgrad_o, table, picks, feats, amat, probs, slope,
    img, cw, mw, xin, y1, y2, wd, bins, pillars, counts, lw, cot,
    wdp, sums, low, row_id, codes, routes, sendbuf,
    rp1, rp2, rp3, rm1, rm2, rm3, win, lidwin, cotwin,
    local_sem, image_sem, send_sem, recv_sem,
):
    me = lax.axis_index(AXES[0]) * strips + lax.axis_index(AXES[1])
    ch_rows = CH * height
    lanes = wdp.shape[0]

    def dev(d):
        t = lax.rem(me + d + n, n)
        return (t // strips, t % strips)

    barrier = pltpu.get_barrier_semaphore()
    for d in (1, 2, 3, -1, -2, -3):
        pl.semaphore_signal(
            barrier, inc=1, device_id=dev(d), device_id_type=pl.DeviceIdType.MESH
        )
    layers = cw.shape[0]
    blocks = range(0, height, BLOCK)
    chunks = [
        pltpu.make_async_copy(
            img_hbm.at[pl.ds(h0, BLOCK)], img.at[pl.ds(h0, BLOCK)], image_sem.at[i]
        )
        for i, h0 in enumerate(blocks)
    ]
    fetches = [
        pltpu.make_async_copy(cw_hbm.at[k], cw.at[k], local_sem.at[k]) for k in range(layers)
    ]
    fetches.append(pltpu.make_async_copy(mw_hbm, mw, local_sem.at[layers]))
    small = [
        pltpu.make_async_copy(src, dst, local_sem.at[layers + 1 + i])
        for i, (src, dst) in enumerate(
            (
                (bins_hbm, bins), (pillars_hbm, pillars), (counts_hbm, counts), (lw_hbm, lw),
                (cot_hbm, cot), (wd_hbm, wd),
            )
        )
    ]
    for copy in (small[0], *chunks, fetches[0], *small[1:]):
        copy.start()
    row_id[...] = row_numbers(row_id.shape)
    wdp[...] = jnp.zeros_like(wdp)
    codes[...] = jnp.full(codes.shape, -1.0, jnp.float32)
    win[...] = jnp.zeros_like(win)
    sec = ba * br
    cot_own, lid_own = (ba + 1) * br, (ba + 2) * br
    small[0].wait()
    cell = br * ba
    sh_cell, sh_ba, sh_br = cell.bit_length() - 1, ba.bit_length() - 1, br.bit_length() - 1
    raw = bins[...]
    off = (raw >> sh_cell) - me + 1
    off = jnp.where(off < 0, off + n, off)
    off = jnp.where(off >= n, off - n, off)
    in_cell = raw & (cell - 1)
    code = (((off << sh_ba) + (in_cell & (ba - 1))) << sh_br) + (in_cell >> sh_ba)
    codes[:, 0:bins_n] = code.astype(jnp.float32)
    turned_codes = jnp.transpose(codes[...])
    turn = block_turn()
    for copy, h0 in zip(chunks, blocks):
        copy.wait()
        for j0 in range(0, cols, BLOCK):
            block = img[h0 : h0 + BLOCK, j0 : j0 + BLOCK, :].reshape(BLOCK * BLOCK, -1)
            turned = jnp.dot(turn, block, preferred_element_type=jnp.float32)
            turned = turned.astype(jnp.bfloat16)
            for c in range(BLOCK):
                at = (3 + j0 + c) * height + h0
                xin[pl.ds(at, BLOCK), :] = turned[c * BLOCK : (c + 1) * BLOCK]
    for copy in fetches[1:]:
        copy.start()
    fetches[0].wait()

    cells = lax.broadcasted_iota(jnp.int32, routes.shape[1:], 1)
    cells = cells.astype(jnp.float32).astype(jnp.bfloat16)

    def route(j):
        code = jnp.broadcast_to(turned_codes[:, j : j + 1], cells.shape).astype(jnp.bfloat16)
        routes[j] = one_hot(code == cells)

    def interior(src, dst, layer, first, last, beside=None):
        for c in range(first, last, 4 * CH):
            if beside is not None:
                for j in range(c - first, min(c - first + 4 * CH, cols)):
                    beside(j)
            at, size = c * height, (min(c + 4 * CH, last) - c) * height
            dst[pl.ds(at, size), :] = conv_rows(src, [(at, size)], cw, layer, height)

    full = cols // CH
    interior(xin, y1, 0, 3, cols + 1, route)
    pl.semaphore_wait(barrier, 6)

    messages = []

    def send(src, dst, d):
        m = len(messages)
        copy = pltpu.make_async_remote_copy(
            src_ref=src,
            dst_ref=dst,
            send_sem=send_sem.at[m],
            recv_sem=recv_sem.at[m],
            device_id=dev(d),
            device_id_type=pl.DeviceIdType.MESH,
        )
        copy.start()
        messages.append(copy)

    h3 = 3 * height
    send(xin.at[pl.ds(cols * height, h3)], xin.at[pl.ds(0, h3)], 1)
    send(xin.at[pl.ds(h3, h3)], xin.at[pl.ds((cols + 3) * height, h3)], -1)
    for copy in small[1:]:
        copy.wait()
    wdp[0:bins_n, :] = wd[...]
    cot_f = cot[...].astype(jnp.float32)
    for a in range(ba):
        cotwin[pl.ds(cot_own + a * br, br), :] = cot_f[:, a, :].astype(jnp.bfloat16)

    def spread(window, start, edge):
        mine = window.at[pl.ds(start, sec)]
        send(mine, window.at[pl.ds(edge, sec)], 1)
        send(mine, window.at[pl.ds(start + sec, sec)], -1)
        last = window.at[pl.ds(start + sec - edge, edge)]
        send(last, window.at[pl.ds(0, edge)], 2)
        send(window.at[pl.ds(start, edge)], window.at[pl.ds(start + 2 * sec, edge)], -2)

    spread(cotwin, cot_own, br)

    fetches[1].wait()
    interior(y1, y2, 1, 3, cols - 1)
    fetches[2].wait()
    messages[0].wait_recv()
    messages[1].wait_recv()

    def edge(layer, src, dst, extra, done):
        right = (3 + done) * height
        size = (cols + extra) * height - right
        both = conv_rows(src, [(0, h3), (right, size)], cw, layer, height)
        dst[pl.ds(0, h3), :] = both[:h3]
        dst[pl.ds(right, size), :] = both[h3:]

    def middle(i):
        at, size = (3 + 2 * CH * i) * height, 2 * CH * height
        feats[pl.ds(at, size), :] = conv_rows(y2, [(at, size)], cw, 2, height)

    inner = full // 2 - 1
    edge(0, xin, y1, 4, cols - 2)
    for i in range(inner):
        middle(i)
        if i == 0:
            points = counts[...]
            scale = (points > 0).astype(jnp.float32) / jnp.maximum(points, 1).astype(jnp.float32)
            pil = pillars[...].astype(jnp.float32)
            pil = jnp.concatenate(
                [pil[k] * scale[:, k : k + 1] for k in range(2 * br)], axis=0
            ).astype(jnp.bfloat16)
            lb, la = br.bit_length() - 1, ba.bit_length() - 1

            def pillar_row(p):
                r, a, uv = p & (br - 1), (p >> lb) & (ba - 1), p >> (lb + la)
                return ((2 * r + (uv >> 1)) << (la + 1)) + 2 * a + (uv & 1)

            gathered = jnp.dot(
                one_hot_rows(4 * sec, 4 * sec, pillar_row), pil, preferred_element_type=jnp.float32
            ).astype(jnp.bfloat16)
            taps = jnp.concatenate([gathered[k * sec : (k + 1) * sec] for k in range(4)], axis=1)
            lid = jnp.dot(
                taps, lw[...].reshape(taps.shape[1], -1), preferred_element_type=jnp.float32
            )
            lidwin[pl.ds(lid_own, sec), :] = jnp.maximum(lid, 0.0).astype(jnp.bfloat16)
            edge(1, y1, y2, 2, cols - 4)
    edge(2, y2, feats, 0, cols - 2 * CH)
    spread(lidwin, lid_own, 2 * br)
    used = 3 * ba * br
    wide = 2 * CH * height
    lane = lax.broadcasted_iota(jnp.int32, (wide, lanes), 1)
    for at in range(0, cols * height, wide):
        rows = pl.ds(at, wide)
        logits = lax.dot_general(
            feats[rows, :], wdp[...], (((1,), (1,)), ((), ())), preferred_element_type=jnp.float32
        )
        e = jnp.exp(-jnp.abs(logits))
        soft = jnp.maximum(logits, 0.0) + jnp.log(1.0 + e) + 0.05
        soft = jnp.where(lane < bins_n, soft, 0.0)
        inv = 1.0 / jnp.sum(soft, axis=1, keepdims=True)
        p = soft * inv
        probs[rows, :] = p
        slope[rows, :] = logits
        sums[rows, :] = inv
        low[rows, :] = p.astype(jnp.bfloat16)
    for j in range(cols):
        rows = pl.ds(j * height, height)
        a = jnp.dot(low[rows, :], routes[j], preferred_element_type=jnp.float32)
        amat[rows, :] = a.astype(jnp.bfloat16)
    mine = lax.dot_general(
        amat[...], feats[...], (((0,), (0,)), ((), ())), preferred_element_type=jnp.float32
    )
    sendbuf[...] = mine.astype(jnp.bfloat16)
    n1, n2, n3 = (2 * ba + 2) * br, (ba + 2) * br, 2 * br
    send(sendbuf.at[pl.ds(used - n1, n1)], rp1, 1)
    send(sendbuf.at[pl.ds(0, n1)], rm1, -1)
    send(sendbuf.at[pl.ds(used - n2, n2)], rp2, 2)
    send(sendbuf.at[pl.ds(0, n2)], rm2, -2)
    send(sendbuf.at[pl.ds(used - n3, n3)], rp3, 3)
    send(sendbuf.at[pl.ds(0, n3)], rm3, -3)

    for at in range(0, cols * height, wide):
        rows = pl.ds(at, wide)
        sig = jax.nn.sigmoid(slope[rows, :]) * sums[rows, :]
        slope[rows, :] = jnp.where(lane < bins_n, sig, 0.0)
    for j in range(0, cols, 2):
        picks[j // 2] = jnp.concatenate(
            [pick_of(row_id, codes, j), pick_of(row_id, codes, j + 1)], axis=1
        )
    for copy in messages[2:10]:
        copy.wait_recv()
    fetches[layers].wait()
    channels = feats.shape[1]
    total = win.shape[0]
    act_rows = total - 2 * br

    def merge(source, lo, hi):
        x = jnp.concatenate([source[i * br : i * br + act_rows] for i in range(3)], axis=1)
        z = [
            jnp.dot(
                x,
                mw[3 * dy : 3 * dy + 3, lo:hi, :].reshape(3 * (hi - lo), -1),
                preferred_element_type=jnp.float32,
            )
            for dy in range(3)
        ]
        return rolled_sum(z[0], z[1], z[2], br)

    lid_act = merge(lidwin[...], channels, mw.shape[1])
    win[pl.ds(2 * br, used), :] = mine
    for copy in messages[10:]:
        copy.wait_recv()
    for got, size in ((rp1, n1), (rp2, n2), (rp3, n3)):
        win[pl.ds(0, size), :] += got[...].astype(jnp.float32)
    for got, size in ((rm1, n1), (rm2, n2), (rm3, n3)):
        win[pl.ds(total - size, size), :] += got[...].astype(jnp.float32)

    act = lid_act + merge(win[...].astype(jnp.bfloat16), 0, channels)
    gate = 1.0 / (1.0 + jnp.exp(-act))
    merged = (act * gate)[cot_own : cot_own + sec]
    merged_o[...] = jnp.stack(
        [merged[a * br : (a + 1) * br] for a in range(ba)], axis=1
    ).astype(jnp.bfloat16)
    grad_pre = (
        cotwin[...].astype(jnp.float32) * (gate * (1.0 + act * (1.0 - gate)))
    ).astype(jnp.bfloat16)

    def merge_back(first, rows, lo, hi):
        y = []
        for dy in range(3):
            acc = None
            for i in range(3):
                term = lax.dot_general(
                    grad_pre[first + (2 - i) * br : first + (2 - i) * br + rows],
                    mw[3 * dy + i, lo:hi, :],
                    (((1,), (1,)), ((), ())),
                    preferred_element_type=jnp.float32,
                )
                acc = term if acc is None else acc + term
            y.append(acc)
        return rolled_sum(y[2], y[1], y[0], br)

    table[...] = merge_back(0, used, 0, channels).astype(jnp.bfloat16)
    lid_grad = merge_back(sec, sec, channels, mw.shape[1])
    lidgrad_o[...] = jnp.stack(
        [lid_grad[a * br : (a + 1) * br] for a in range(ba)], axis=1
    ).astype(jnp.bfloat16)
    for copy in messages:
        copy.wait_send()


def back_kernel(
    height, bins_n, steps,
    feats, amat, probs, slope, picks, table, wd, merged, lid_grad,
    camgrad_o, merged_o, lidgrad_o,
    wdp, seen, gprobs, buf, sem,
):
    lanes = wdp.shape[0]
    copies = [
        pltpu.make_async_copy(merged, merged_o, sem.at[0]),
        pltpu.make_async_copy(lid_grad, lidgrad_o, sem.at[1]),
    ]
    for copy in copies:
        copy.start()
    wdp[...] = jnp.zeros_like(wdp)
    wdp[0:bins_n, :] = wd[...]
    turn = block_turn()
    tab = table[...]
    seen[...] = lax.dot_general(
        feats[...], tab, (((1,), (1,)), ((), ())), preferred_element_type=jnp.float32
    ).astype(jnp.bfloat16)
    for pair in range(picks.shape[0]):
        at = 2 * pair * height
        both = jnp.dot(
            seen[pl.ds(at, 2 * height), :], picks[pair], preferred_element_type=jnp.float32
        )
        gprobs[pl.ds(at, height), :] = both[:height, :lanes]
        gprobs[pl.ds(at + height, height), :] = both[height:, lanes:]
    wide = BLOCK * height
    for step in range(steps):
        rows = pl.ds(step * wide, wide)
        gp = gprobs[rows, :]
        mean = jnp.sum(gp * probs[rows, :], axis=1, keepdims=True)
        gl = ((gp - mean) * slope[rows, :]).astype(jnp.bfloat16)
        direct = jnp.dot(amat[rows, :], tab, preferred_element_type=jnp.float32)
        depth = jnp.dot(gl, wdp[...], preferred_element_type=jnp.float32)
        block = (direct + depth).astype(jnp.bfloat16)
        for k, h0 in enumerate(range(0, height, BLOCK)):
            part = jnp.concatenate(
                [block[c * height + h0 : c * height + h0 + BLOCK] for c in range(BLOCK)], axis=0
            )
            turned = jnp.dot(turn, part, preferred_element_type=jnp.float32)
            spot = (pl.ds(h0, BLOCK), pl.ds(step * BLOCK, BLOCK))
            buf[spot] = turned.astype(jnp.bfloat16).reshape(BLOCK, BLOCK, -1)
            copy = pltpu.make_async_copy(
                buf.at[spot], camgrad_o.at[spot], sem.at[2 + step * (height // BLOCK) + k]
            )
            copy.start()
            copies.append(copy)
    for copy in copies:
        copy.wait()


def local(
    n, strips,
    image_feats, cam_weights, depth_weight, ray_bins, pillar_sums, pillar_counts,
    lidar_weight, merge_weight, out_cotangent,
):
    height, cols, channels = image_feats.shape
    br, ba, cf = out_cotangent.shape
    bins_n = depth_weight.shape[1]
    cl = pillar_sums.shape[2]
    lanes = -(-bins_n // 128) * 128
    used = groups = 3 * ba * br
    total = (3 * ba + 4) * br
    bf, f32 = jnp.bfloat16, jnp.float32

    vm = pl.BlockSpec(memory_space=pltpu.VMEM)
    hbm = pl.BlockSpec(memory_space=pltpu.HBM)
    n1, n2, n3 = (2 * ba + 2) * br, (ba + 2) * br, 2 * br
    rows = cols * height
    turned_counts = pillar_counts.T
    turned_depth = depth_weight.T
    merged, lid_grad, table, picks, feats, amat, probs, slope = pl.pallas_call(
        functools.partial(kernel, n, strips, cols, height, br, ba, bins_n),
        out_shape=(
            pltpu.VMEM((br, ba, cf), bf),
            pltpu.VMEM((br, ba, cl), bf),
            pltpu.VMEM((groups, channels), bf),
            pltpu.VMEM((cols // 2, groups, 2 * lanes), bf),
            pltpu.VMEM((rows, channels), bf),
            pltpu.VMEM((rows, groups), bf),
            pltpu.VMEM((rows, lanes), f32),
            pltpu.VMEM((rows, lanes), f32),
        ),
        in_specs=[hbm] * 9,
        out_specs=(vm,) * 8,
        scratch_shapes=[
            pltpu.VMEM(image_feats.shape, bf),
            pltpu.VMEM(cam_weights.shape, bf),
            pltpu.VMEM(merge_weight.shape, bf),
            pltpu.VMEM(((cols + 6) * height, channels), bf),
            pltpu.VMEM(((cols + 4) * height, channels), bf),
            pltpu.VMEM(((cols + 2) * height, channels), bf),
            pltpu.VMEM(turned_depth.shape, bf),
            pltpu.VMEM(ray_bins.shape, jnp.int32),
            pltpu.VMEM(pillar_sums.shape, bf),
            pltpu.VMEM(turned_counts.shape, jnp.int32),
            pltpu.VMEM(lidar_weight.shape, bf),
            pltpu.VMEM(out_cotangent.shape, bf),
            pltpu.VMEM((lanes, channels), bf),
            pltpu.VMEM((cols * height, 1), f32),
            pltpu.VMEM((cols * height, lanes), bf),
            pltpu.VMEM((groups, lanes), bf),
            pltpu.VMEM((cols, lanes), f32),
            pltpu.VMEM((cols, lanes, groups), bf),
            pltpu.VMEM((used, channels), bf),
            pltpu.VMEM((n1, channels), bf),
            pltpu.VMEM((n2, channels), bf),
            pltpu.VMEM((n3, channels), bf),
            pltpu.VMEM((n1, channels), bf),
            pltpu.VMEM((n2, channels), bf),
            pltpu.VMEM((n3, channels), bf),
            pltpu.VMEM((total, channels), f32),
            pltpu.VMEM((total, cl), bf),
            pltpu.VMEM((total - 2 * br, cf), bf),
            pltpu.SemaphoreType.DMA((cam_weights.shape[0] + 7,)),
            pltpu.SemaphoreType.DMA((height // BLOCK,)),
            pltpu.SemaphoreType.DMA((16,)),
            pltpu.SemaphoreType.DMA((16,)),
        ],
        compiler_params=pltpu.CompilerParams(
            collective_id=0, has_side_effects=True, vmem_limit_bytes=44 * 1024 * 1024
        ),
        name="bev",
    )(
        *(
            pltpu.with_memory_space_constraint(x, pltpu.HBM)
            for x in (
                image_feats, cam_weights, turned_depth, ray_bins, pillar_sums, turned_counts,
                lidar_weight, out_cotangent, merge_weight,
            )
        )
    )
    steps = cols // BLOCK
    cam_grad, merged, lid_grad = pl.pallas_call(
        functools.partial(back_kernel, height, bins_n, steps),
        out_shape=(
            pltpu.HBM((height, cols, channels), bf),
            pltpu.HBM((br, ba, cf), bf),
            pltpu.HBM((br, ba, cl), bf),
        ),
        in_specs=[vm] * 9,
        out_specs=(hbm,) * 3,
        scratch_shapes=[
            pltpu.VMEM((lanes, channels), bf),
            pltpu.VMEM((rows, groups), bf),
            pltpu.VMEM((rows, lanes), f32),
            pltpu.VMEM((height, cols, channels), bf),
            pltpu.SemaphoreType.DMA((2 + steps * (height // BLOCK),)),
        ],
        compiler_params=pltpu.CompilerParams(vmem_limit_bytes=20 * 1024 * 1024),
        name="back",
    )(feats, amat, probs, slope, picks, table, turned_depth, merged, lid_grad)
    return merged, cam_grad, lid_grad


def solution(mesh):
    strips = mesh.shape["strip"]
    n = mesh.shape["branch"] * strips
    placed = (
        P(None, AXES, None),
        P(),
        P(),
        P(AXES, None),
        P(None, AXES, None),
        P(None, AXES),
        P(),
        P(),
        P(None, AXES, None),
    )
    return jax.shard_map(
        functools.partial(local, n, strips),
        mesh=mesh,
        in_specs=placed,
        out_specs=(P(None, AXES, None),) * 3,
        check_vma=False,
    )
```

```python
import functools

import jax
import jax.numpy as jnp
from jax import lax
from jax.experimental import pallas as pl
from jax.experimental.pallas import tpu as pltpu
from jax.sharding import PartitionSpec as P

AXES = ("branch", "strip")
CH = 8
BLOCK = 16


def rolled_sum(low, mid, high, period):
    rows = mid.shape[0]
    place = lax.broadcasted_iota(jnp.int32, mid.shape, 0) & (period - 1)
    down = jnp.where(place == 0, 0.0, pltpu.roll(low, 1, 0))
    up = jnp.where(place == period - 1, 0.0, pltpu.roll(high, rows - 1, 0))
    return mid + down + up


def conv_rows(src, pieces, weights, layer, height):
    taps = [
        jnp.concatenate([src[pl.ds(s + i * height, rows), :] for s, rows in pieces], axis=0)
        for i in range(3)
    ]
    x = jnp.concatenate(taps, axis=1)
    channels = taps[0].shape[1]
    z = [
        jnp.dot(
            x,
            weights[layer, 3 * dy : 3 * dy + 3].reshape(3 * channels, -1),
            preferred_element_type=jnp.float32,
        )
        for dy in range(3)
    ]
    total = rolled_sum(z[0], z[1], z[2], height)
    return jnp.maximum(total, 0.0).astype(jnp.bfloat16)


def one_hot_rows(rows, sources, source_of):
    p = lax.broadcasted_iota(jnp.int32, (rows, sources), 0)
    q = lax.broadcasted_iota(jnp.int32, (rows, sources), 1)
    return jnp.where(source_of(p) == q, 1.0, 0.0).astype(jnp.bfloat16)


def row_numbers(shape):
    return lax.broadcasted_iota(jnp.int32, shape, 0).astype(jnp.float32).astype(jnp.bfloat16)


def one_hot(hit):
    return jnp.where(hit, jnp.ones((), jnp.bfloat16), jnp.zeros((), jnp.bfloat16))


def pick_of(row_id, codes, j):
    groups, lanes = row_id.shape
    code = jnp.broadcast_to(codes[pl.ds(j, 1), :], (16, lanes)).astype(jnp.bfloat16)
    code = jnp.concatenate([code] * (groups // 16), axis=0)
    return one_hot(row_id[...] == code)


def block_turn():
    shift = BLOCK.bit_length() - 1
    return one_hot_rows(
        BLOCK * BLOCK,
        BLOCK * BLOCK,
        lambda p: ((p & (BLOCK - 1)) << shift) + (p >> shift),
    )


def kernel(
    n, strips, cols, height, br, ba, bins_n,
    img_hbm, cw_hbm, wd_hbm, bins_hbm, pillars_hbm, counts_hbm, lw_hbm, cot_hbm, mw_hbm,
    merged_o, lidgrad_o, table, picks, feats, amat, probs, slope,
    img, cw, mw, xin, y1, y2, wd, bins, pillars, counts, lw, cot,
    wdp, sums, low, row_id, codes, routes, sendbuf,
    rp1, rp2, rp3, rm1, rm2, rm3, win, lidwin, cotwin,
    local_sem, image_sem, send_sem, recv_sem,
):
    me = lax.axis_index(AXES[0]) * strips + lax.axis_index(AXES[1])
    ch_rows = CH * height
    lanes = wdp.shape[0]

    def dev(d):
        t = lax.rem(me + d + n, n)
        return (t // strips, t % strips)

    barrier = pltpu.get_barrier_semaphore()
    for d in (1, 2, 3, -1, -2, -3):
        pl.semaphore_signal(
            barrier, inc=1, device_id=dev(d), device_id_type=pl.DeviceIdType.MESH
        )
    layers = cw.shape[0]
    blocks = range(0, height, BLOCK)
    half = BLOCK // 2
    chunks = [
        pltpu.make_async_copy(img_hbm.at[pl.ds(h0, half)], img.at[pl.ds(h0, half)], image_sem.at[i])
        for i, h0 in enumerate(range(0, height, half))
    ]
    fetches = [
        pltpu.make_async_copy(cw_hbm.at[k], cw.at[k], local_sem.at[k]) for k in range(layers)
    ]
    fetches.append(pltpu.make_async_copy(mw_hbm, mw, local_sem.at[layers]))
    small = [
        pltpu.make_async_copy(src, dst, local_sem.at[layers + 1 + i])
        for i, (src, dst) in enumerate(
            (
                (bins_hbm, bins), (pillars_hbm, pillars), (counts_hbm, counts), (lw_hbm, lw),
                (cot_hbm, cot), (wd_hbm, wd),
            )
        )
    ]
    for copy in (*chunks, small[0], fetches[0]):
        copy.start()
    row_id[...] = row_numbers(row_id.shape)
    wdp[...] = jnp.zeros_like(wdp)
    codes[...] = jnp.full(codes.shape, -1.0, jnp.float32)
    win[...] = jnp.zeros_like(win)
    sec = ba * br
    cot_own, lid_own = (ba + 1) * br, (ba + 2) * br
    small[0].wait()
    cell = br * ba
    sh_cell, sh_ba, sh_br = cell.bit_length() - 1, ba.bit_length() - 1, br.bit_length() - 1
    raw = bins[...]
    off = (raw >> sh_cell) - me + 1
    off = jnp.where(off < 0, off + n, off)
    off = jnp.where(off >= n, off - n, off)
    in_cell = raw & (cell - 1)
    code = (((off << sh_ba) + (in_cell & (ba - 1))) << sh_br) + (in_cell >> sh_ba)
    codes[:, 0:bins_n] = code.astype(jnp.float32)
    turned_codes = jnp.transpose(codes[...])
    turn = block_turn()
    for i, h0 in enumerate(blocks):
        chunks[2 * i].wait()
        chunks[2 * i + 1].wait()
        for j0 in range(0, cols, BLOCK):
            block = img[h0 : h0 + BLOCK, j0 : j0 + BLOCK, :].reshape(BLOCK * BLOCK, -1)
            turned = jnp.dot(turn, block, preferred_element_type=jnp.float32)
            turned = turned.astype(jnp.bfloat16)
            for c in range(BLOCK):
                at = (3 + j0 + c) * height + h0
                xin[pl.ds(at, BLOCK), :] = turned[c * BLOCK : (c + 1) * BLOCK]
    for copy in (*small[1:], *fetches[1:]):
        copy.start()
    fetches[0].wait()

    cells = lax.broadcasted_iota(jnp.int32, routes.shape[1:], 1)
    cells = cells.astype(jnp.float32).astype(jnp.bfloat16)

    def route(j):
        code = jnp.broadcast_to(turned_codes[:, j : j + 1], cells.shape).astype(jnp.bfloat16)
        routes[j] = one_hot(code == cells)

    def interior(src, dst, layer, first, last, beside=None):
        for c in range(first, last, 4 * CH):
            if beside is not None:
                for j in range(c - first, min(c - first + 4 * CH, cols)):
                    beside(j)
            at, size = c * height, (min(c + 4 * CH, last) - c) * height
            dst[pl.ds(at, size), :] = conv_rows(src, [(at, size)], cw, layer, height)

    full = cols // CH
    interior(xin, y1, 0, 3, cols + 1, route)
    pl.semaphore_wait(barrier, 6)

    messages = []

    def send(src, dst, d):
        m = len(messages)
        copy = pltpu.make_async_remote_copy(
            src_ref=src,
            dst_ref=dst,
            send_sem=send_sem.at[m],
            recv_sem=recv_sem.at[m],
            device_id=dev(d),
            device_id_type=pl.DeviceIdType.MESH,
        )
        copy.start()
        messages.append(copy)

    h3 = 3 * height
    send(xin.at[pl.ds(cols * height, h3)], xin.at[pl.ds(0, h3)], 1)
    send(xin.at[pl.ds(h3, h3)], xin.at[pl.ds((cols + 3) * height, h3)], -1)
    for copy in small[1:]:
        copy.wait()
    wdp[0:bins_n, :] = wd[...]
    cot_f = cot[...].astype(jnp.float32)
    for a in range(ba):
        cotwin[pl.ds(cot_own + a * br, br), :] = cot_f[:, a, :].astype(jnp.bfloat16)

    def spread(window, start, edge):
        mine = window.at[pl.ds(start, sec)]
        send(mine, window.at[pl.ds(edge, sec)], 1)
        send(mine, window.at[pl.ds(start + sec, sec)], -1)
        last = window.at[pl.ds(start + sec - edge, edge)]
        send(last, window.at[pl.ds(0, edge)], 2)
        send(window.at[pl.ds(start, edge)], window.at[pl.ds(start + 2 * sec, edge)], -2)

    spread(cotwin, cot_own, br)

    fetches[1].wait()
    interior(y1, y2, 1, 3, cols - 1)
    fetches[2].wait()
    messages[0].wait_recv()
    messages[1].wait_recv()

    def edge(layer, src, dst, extra, done):
        right = (3 + done) * height
        size = (cols + extra) * height - right
        both = conv_rows(src, [(0, h3), (right, size)], cw, layer, height)
        dst[pl.ds(0, h3), :] = both[:h3]
        dst[pl.ds(right, size), :] = both[h3:]

    def middle(i):
        at, size = (3 + 2 * CH * i) * height, 2 * CH * height
        feats[pl.ds(at, size), :] = conv_rows(y2, [(at, size)], cw, 2, height)

    inner = full // 2 - 1
    edge(0, xin, y1, 4, cols - 2)
    for i in range(inner):
        middle(i)
        if i == 0:
            points = counts[...]
            scale = (points > 0).astype(jnp.float32) / jnp.maximum(points, 1).astype(jnp.float32)
            pil = pillars[...].astype(jnp.float32)
            pil = jnp.concatenate(
                [pil[k] * scale[:, k : k + 1] for k in range(2 * br)], axis=0
            ).astype(jnp.bfloat16)
            lb, la = br.bit_length() - 1, ba.bit_length() - 1

            def pillar_row(p):
                r, a, uv = p & (br - 1), (p >> lb) & (ba - 1), p >> (lb + la)
                return ((2 * r + (uv >> 1)) << (la + 1)) + 2 * a + (uv & 1)

            gathered = jnp.dot(
                one_hot_rows(4 * sec, 4 * sec, pillar_row), pil, preferred_element_type=jnp.float32
            ).astype(jnp.bfloat16)
            taps = jnp.concatenate([gathered[k * sec : (k + 1) * sec] for k in range(4)], axis=1)
            lid = jnp.dot(
                taps, lw[...].reshape(taps.shape[1], -1), preferred_element_type=jnp.float32
            )
            lidwin[pl.ds(lid_own, sec), :] = jnp.maximum(lid, 0.0).astype(jnp.bfloat16)
            edge(1, y1, y2, 2, cols - 4)
    edge(2, y2, feats, 0, cols - 2 * CH)
    spread(lidwin, lid_own, 2 * br)
    used = 3 * ba * br
    wide = 2 * CH * height
    lane = lax.broadcasted_iota(jnp.int32, (wide, lanes), 1)

    def soften(at):
        rows = pl.ds(at, wide)
        logits = lax.dot_general(
            feats[rows, :], wdp[...], (((1,), (1,)), ((), ())), preferred_element_type=jnp.float32
        )
        e = jnp.exp(-jnp.abs(logits))
        soft = jnp.maximum(logits, 0.0) + jnp.log(1.0 + e) + 0.05
        soft = jnp.where(lane < bins_n, soft, 0.0)
        inv = 1.0 / jnp.sum(soft, axis=1, keepdims=True)
        p = soft * inv
        probs[rows, :] = p
        slope[rows, :] = logits
        sums[rows, :] = inv
        low[rows, :] = p.astype(jnp.bfloat16)

    def lift(at):
        for row in range(at, at + wide, height):
            rows = pl.ds(row, height)
            a = jnp.dot(low[rows, :], routes[row // height], preferred_element_type=jnp.float32)
            amat[rows, :] = a.astype(jnp.bfloat16)

    soften(0)
    for at in range(0, cols * height, wide):
        if at + wide < cols * height:
            soften(at + wide)
        lift(at)
    mine = lax.dot_general(
        amat[...], feats[...], (((0,), (0,)), ((), ())), preferred_element_type=jnp.float32
    )
    sendbuf[...] = mine.astype(jnp.bfloat16)
    n1, n2, n3 = (2 * ba + 2) * br, (ba + 2) * br, 2 * br
    send(sendbuf.at[pl.ds(used - n3, n3)], rp3, 3)
    send(sendbuf.at[pl.ds(0, n3)], rm3, -3)
    send(sendbuf.at[pl.ds(used - n2, n2)], rp2, 2)
    send(sendbuf.at[pl.ds(0, n2)], rm2, -2)
    send(sendbuf.at[pl.ds(used - n1, n1)], rp1, 1)
    send(sendbuf.at[pl.ds(0, n1)], rm1, -1)
    for at in range(0, cols * height, wide):
        rows = pl.ds(at, wide)
        sig = jax.nn.sigmoid(slope[rows, :]) * sums[rows, :]
        slope[rows, :] = jnp.where(lane < bins_n, sig, 0.0)
    for j in range(0, cols, 2):
        picks[j // 2] = jnp.concatenate(
            [pick_of(row_id, codes, j), pick_of(row_id, codes, j + 1)], axis=1
        )
    for copy in messages[2:10]:
        copy.wait_recv()
    fetches[layers].wait()
    channels = feats.shape[1]
    total = win.shape[0]
    act_rows = total - 2 * br

    def merge(source, lo, hi):
        x = jnp.concatenate([source[i * br : i * br + act_rows] for i in range(3)], axis=1)
        z = [
            jnp.dot(
                x,
                mw[3 * dy : 3 * dy + 3, lo:hi, :].reshape(3 * (hi - lo), -1),
                preferred_element_type=jnp.float32,
            )
            for dy in range(3)
        ]
        return rolled_sum(z[0], z[1], z[2], br)

    lid_act = merge(lidwin[...], channels, mw.shape[1])
    win[pl.ds(2 * br, used), :] = mine
    for copy in messages[10:]:
        copy.wait_recv()
    for got, size in ((rp1, n1), (rp2, n2), (rp3, n3)):
        win[pl.ds(0, size), :] += got[...].astype(jnp.float32)
    for got, size in ((rm1, n1), (rm2, n2), (rm3, n3)):
        win[pl.ds(total - size, size), :] += got[...].astype(jnp.float32)

    act = lid_act + merge(win[...].astype(jnp.bfloat16), 0, channels)
    gate = 1.0 / (1.0 + jnp.exp(-act))
    merged = (act * gate)[cot_own : cot_own + sec]
    merged_o[...] = jnp.stack(
        [merged[a * br : (a + 1) * br] for a in range(ba)], axis=1
    ).astype(jnp.bfloat16)
    grad_pre = (
        cotwin[...].astype(jnp.float32) * (gate * (1.0 + act * (1.0 - gate)))
    ).astype(jnp.bfloat16)

    def merge_back(first, rows, lo, hi):
        y = []
        for dy in range(3):
            acc = None
            for i in range(3):
                term = lax.dot_general(
                    grad_pre[first + (2 - i) * br : first + (2 - i) * br + rows],
                    mw[3 * dy + i, lo:hi, :],
                    (((1,), (1,)), ((), ())),
                    preferred_element_type=jnp.float32,
                )
                acc = term if acc is None else acc + term
            y.append(acc)
        return rolled_sum(y[2], y[1], y[0], br)

    table[...] = merge_back(0, used, 0, channels).astype(jnp.bfloat16)
    lid_grad = merge_back(sec, sec, channels, mw.shape[1])
    lidgrad_o[...] = jnp.stack(
        [lid_grad[a * br : (a + 1) * br] for a in range(ba)], axis=1
    ).astype(jnp.bfloat16)
    for copy in messages:
        copy.wait_send()


def back_kernel(
    height, bins_n, steps,
    feats, amat, probs, slope, picks, table, wd, merged, lid_grad,
    camgrad_o, merged_o, lidgrad_o,
    wdp, seen, gprobs, glog, buf, sem,
):
    lanes = wdp.shape[0]
    copies = [
        pltpu.make_async_copy(merged, merged_o, sem.at[0]),
        pltpu.make_async_copy(lid_grad, lidgrad_o, sem.at[1]),
    ]
    for copy in copies:
        copy.start()
    wdp[...] = jnp.zeros_like(wdp)
    wdp[0:bins_n, :] = wd[...]
    turn = block_turn()
    tab = table[...]
    seen[...] = lax.dot_general(
        feats[...], tab, (((1,), (1,)), ((), ())), preferred_element_type=jnp.float32
    ).astype(jnp.bfloat16)
    for pair in range(picks.shape[0]):
        at = 2 * pair * height
        both = jnp.dot(
            seen[pl.ds(at, 2 * height), :], picks[pair], preferred_element_type=jnp.float32
        )
        gprobs[pl.ds(at, height), :] = both[:height, :lanes]
        gprobs[pl.ds(at + height, height), :] = both[height:, lanes:]
    gp = gprobs[...]
    mean = jnp.sum(gp * probs[...], axis=1, keepdims=True)
    glog[...] = ((gp - mean) * slope[...]).astype(jnp.bfloat16)
    wide = BLOCK * height

    def total(step):
        rows = pl.ds(step * wide, wide)
        direct = jnp.dot(amat[rows, :], tab, preferred_element_type=jnp.float32)
        depth = jnp.dot(glog[rows, :], wdp[...], preferred_element_type=jnp.float32)
        return (direct + depth).astype(jnp.bfloat16)

    blocks = [total(step) for step in range(steps)]
    for k, h0 in enumerate(range(0, height, BLOCK)):
        for step, block in enumerate(blocks):
            part = jnp.concatenate(
                [block[c * height + h0 : c * height + h0 + BLOCK] for c in range(BLOCK)], axis=0
            )
            turned = jnp.dot(turn, part, preferred_element_type=jnp.float32)
            buf[h0 : h0 + BLOCK, pl.ds(step * BLOCK, BLOCK), :] = turned.astype(
                jnp.bfloat16
            ).reshape(BLOCK, BLOCK, -1)
        for q in range(4):
            rows = pl.ds(h0 + q * (BLOCK // 4), BLOCK // 4)
            copy = pltpu.make_async_copy(
                buf.at[rows], camgrad_o.at[rows], sem.at[2 + 4 * k + q]
            )
            copy.start()
            copies.append(copy)
    for copy in copies:
        copy.wait()


def local(
    n, strips,
    image_feats, cam_weights, depth_weight, ray_bins, pillar_sums, pillar_counts,
    lidar_weight, merge_weight, out_cotangent,
):
    height, cols, channels = image_feats.shape
    br, ba, cf = out_cotangent.shape
    bins_n = depth_weight.shape[1]
    cl = pillar_sums.shape[2]
    lanes = -(-bins_n // 128) * 128
    used = groups = 3 * ba * br
    total = (3 * ba + 4) * br
    bf, f32 = jnp.bfloat16, jnp.float32

    vm = pl.BlockSpec(memory_space=pltpu.VMEM)
    hbm = pl.BlockSpec(memory_space=pltpu.HBM)
    n1, n2, n3 = (2 * ba + 2) * br, (ba + 2) * br, 2 * br
    rows = cols * height
    turned_counts = pillar_counts.T
    turned_depth = depth_weight.T
    merged, lid_grad, table, picks, feats, amat, probs, slope = pl.pallas_call(
        functools.partial(kernel, n, strips, cols, height, br, ba, bins_n),
        out_shape=(
            pltpu.VMEM((br, ba, cf), bf),
            pltpu.VMEM((br, ba, cl), bf),
            pltpu.VMEM((groups, channels), bf),
            pltpu.VMEM((cols // 2, groups, 2 * lanes), bf),
            pltpu.VMEM((rows, channels), bf),
            pltpu.VMEM((rows, groups), bf),
            pltpu.VMEM((rows, lanes), f32),
            pltpu.VMEM((rows, lanes), f32),
        ),
        in_specs=[hbm] * 9,
        out_specs=(vm,) * 8,
        scratch_shapes=[
            pltpu.VMEM(image_feats.shape, bf),
            pltpu.VMEM(cam_weights.shape, bf),
            pltpu.VMEM(merge_weight.shape, bf),
            pltpu.VMEM(((cols + 6) * height, channels), bf),
            pltpu.VMEM(((cols + 4) * height, channels), bf),
            pltpu.VMEM(((cols + 2) * height, channels), bf),
            pltpu.VMEM(turned_depth.shape, bf),
            pltpu.VMEM(ray_bins.shape, jnp.int32),
            pltpu.VMEM(pillar_sums.shape, bf),
            pltpu.VMEM(turned_counts.shape, jnp.int32),
            pltpu.VMEM(lidar_weight.shape, bf),
            pltpu.VMEM(out_cotangent.shape, bf),
            pltpu.VMEM((lanes, channels), bf),
            pltpu.VMEM((cols * height, 1), f32),
            pltpu.VMEM((cols * height, lanes), bf),
            pltpu.VMEM((groups, lanes), bf),
            pltpu.VMEM((cols, lanes), f32),
            pltpu.VMEM((cols, lanes, groups), bf),
            pltpu.VMEM((used, channels), bf),
            pltpu.VMEM((n1, channels), bf),
            pltpu.VMEM((n2, channels), bf),
            pltpu.VMEM((n3, channels), bf),
            pltpu.VMEM((n1, channels), bf),
            pltpu.VMEM((n2, channels), bf),
            pltpu.VMEM((n3, channels), bf),
            pltpu.VMEM((total, channels), f32),
            pltpu.VMEM((total, cl), bf),
            pltpu.VMEM((total - 2 * br, cf), bf),
            pltpu.SemaphoreType.DMA((cam_weights.shape[0] + 7,)),
            pltpu.SemaphoreType.DMA((2 * height // BLOCK,)),
            pltpu.SemaphoreType.DMA((16,)),
            pltpu.SemaphoreType.DMA((16,)),
        ],
        compiler_params=pltpu.CompilerParams(
            collective_id=0, has_side_effects=True, vmem_limit_bytes=44 * 1024 * 1024
        ),
        name="bev",
    )(
        *(
            pltpu.with_memory_space_constraint(x, pltpu.HBM)
            for x in (
                image_feats, cam_weights, turned_depth, ray_bins, pillar_sums, turned_counts,
                lidar_weight, out_cotangent, merge_weight,
            )
        )
    )
    steps = cols // BLOCK
    cam_grad, merged, lid_grad = pl.pallas_call(
        functools.partial(back_kernel, height, bins_n, steps),
        out_shape=(
            pltpu.HBM((height, cols, channels), bf),
            pltpu.HBM((br, ba, cf), bf),
            pltpu.HBM((br, ba, cl), bf),
        ),
        in_specs=[vm] * 9,
        out_specs=(hbm,) * 3,
        scratch_shapes=[
            pltpu.VMEM((lanes, channels), bf),
            pltpu.VMEM((rows, groups), bf),
            pltpu.VMEM((rows, lanes), f32),
            pltpu.VMEM((rows, lanes), bf),
            pltpu.VMEM((height, cols, channels), bf),
            pltpu.SemaphoreType.DMA((2 + 4 * (height // BLOCK),)),
        ],
        compiler_params=pltpu.CompilerParams(vmem_limit_bytes=20 * 1024 * 1024),
        name="back",
    )(feats, amat, probs, slope, picks, table, turned_depth, merged, lid_grad)
    return merged, cam_grad, lid_grad


def solution(mesh):
    strips = mesh.shape["strip"]
    n = mesh.shape["branch"] * strips
    placed = (
        P(None, AXES, None),
        P(),
        P(),
        P(AXES, None),
        P(None, AXES, None),
        P(None, AXES),
        P(),
        P(),
        P(None, AXES, None),
    )
    return jax.shard_map(
        functools.partial(local, n, strips),
        mesh=mesh,
        in_specs=placed,
        out_specs=(P(None, AXES, None),) * 3,
        check_vma=False,
    )
```

```python
import functools

import jax
import jax.numpy as jnp
from jax import lax
from jax.experimental import pallas as pl
from jax.experimental.pallas import tpu as pltpu
from jax.sharding import PartitionSpec as P

AXES = ("branch", "strip")
CH = 8
BLOCK = 16


def rolled_sum(low, mid, high, period):
    rows = mid.shape[0]
    place = lax.broadcasted_iota(jnp.int32, mid.shape, 0) & (period - 1)
    down = jnp.where(place == 0, 0.0, pltpu.roll(low, 1, 0))
    up = jnp.where(place == period - 1, 0.0, pltpu.roll(high, rows - 1, 0))
    return mid + down + up


def conv_rows(src, pieces, weights, layer, height):
    taps = [
        jnp.concatenate([src[pl.ds(s + i * height, rows), :] for s, rows in pieces], axis=0)
        for i in range(3)
    ]
    x = jnp.concatenate(taps, axis=1)
    channels = taps[0].shape[1]
    z = [
        jnp.dot(
            x,
            weights[layer, 3 * dy : 3 * dy + 3].reshape(3 * channels, -1),
            preferred_element_type=jnp.float32,
        )
        for dy in range(3)
    ]
    total = rolled_sum(z[0], z[1], z[2], height)
    return jnp.maximum(total, 0.0).astype(jnp.bfloat16)


def one_hot_rows(rows, sources, source_of):
    p = lax.broadcasted_iota(jnp.int32, (rows, sources), 0)
    q = lax.broadcasted_iota(jnp.int32, (rows, sources), 1)
    return jnp.where(source_of(p) == q, 1.0, 0.0).astype(jnp.bfloat16)


def row_numbers(shape):
    return lax.broadcasted_iota(jnp.int32, shape, 0).astype(jnp.float32).astype(jnp.bfloat16)


def one_hot(hit):
    return jnp.where(hit, jnp.ones((), jnp.bfloat16), jnp.zeros((), jnp.bfloat16))


def pick_of(row_id, codes, j):
    groups, lanes = row_id.shape
    code = jnp.broadcast_to(codes[pl.ds(j, 1), :], (16, lanes)).astype(jnp.bfloat16)
    code = jnp.concatenate([code] * (groups // 16), axis=0)
    return one_hot(row_id[...] == code)


def block_turn():
    shift = BLOCK.bit_length() - 1
    return one_hot_rows(
        BLOCK * BLOCK,
        BLOCK * BLOCK,
        lambda p: ((p & (BLOCK - 1)) << shift) + (p >> shift),
    )


def kernel(
    n, strips, cols, height, br, ba, bins_n,
    img_hbm, cw_hbm, wd_hbm, bins_hbm, pillars_hbm, counts_hbm, lw_hbm, cot_hbm, mw_hbm,
    merged_o, lidgrad_o, table, picks, feats, amat, probs, slope,
    img, cw, mw, xin, y1, y2, wd, bins, pillars, counts, lw, cot,
    wdp, sums, low, row_id, codes, routes, sendbuf,
    rp1, rp2, rp3, rm1, rm2, rm3, win, lidwin, cotwin,
    local_sem, image_sem, send_sem, recv_sem,
):
    me = lax.axis_index(AXES[0]) * strips + lax.axis_index(AXES[1])
    ch_rows = CH * height
    lanes = wdp.shape[0]

    def dev(d):
        t = lax.rem(me + d + n, n)
        return (t // strips, t % strips)

    barrier = pltpu.get_barrier_semaphore()
    for d in (1, 2, 3, -1, -2, -3):
        pl.semaphore_signal(
            barrier, inc=1, device_id=dev(d), device_id_type=pl.DeviceIdType.MESH
        )
    layers = cw.shape[0]
    blocks = range(0, height, BLOCK)
    half = BLOCK // 2
    chunks = [
        pltpu.make_async_copy(img_hbm.at[pl.ds(h0, half)], img.at[pl.ds(h0, half)], image_sem.at[i])
        for i, h0 in enumerate(range(0, height, half))
    ]
    fetches = [
        pltpu.make_async_copy(cw_hbm.at[k], cw.at[k], local_sem.at[k]) for k in range(layers)
    ]
    fetches.append(pltpu.make_async_copy(mw_hbm, mw, local_sem.at[layers]))
    small = [
        pltpu.make_async_copy(src, dst, local_sem.at[layers + 1 + i])
        for i, (src, dst) in enumerate(
            (
                (bins_hbm, bins), (pillars_hbm, pillars), (counts_hbm, counts), (lw_hbm, lw),
                (cot_hbm, cot), (wd_hbm, wd),
            )
        )
    ]
    for copy in (*chunks, small[0], fetches[0]):
        copy.start()
    row_id[...] = row_numbers(row_id.shape)
    wdp[...] = jnp.zeros_like(wdp)
    codes[...] = jnp.full(codes.shape, -1.0, jnp.float32)
    win[...] = jnp.zeros_like(win)
    sec = ba * br
    cot_own, lid_own = (ba + 1) * br, (ba + 2) * br
    small[0].wait()
    cell = br * ba
    sh_cell, sh_ba, sh_br = cell.bit_length() - 1, ba.bit_length() - 1, br.bit_length() - 1
    raw = bins[...]
    off = (raw >> sh_cell) - me + 1
    off = jnp.where(off < 0, off + n, off)
    off = jnp.where(off >= n, off - n, off)
    in_cell = raw & (cell - 1)
    code = (((off << sh_ba) + (in_cell & (ba - 1))) << sh_br) + (in_cell >> sh_ba)
    codes[:, 0:bins_n] = code.astype(jnp.float32)
    turned_codes = jnp.transpose(codes[...])
    turn = block_turn()
    for i, h0 in enumerate(blocks):
        chunks[2 * i].wait()
        chunks[2 * i + 1].wait()
        for j0 in range(0, cols, BLOCK):
            block = img[h0 : h0 + BLOCK, j0 : j0 + BLOCK, :].reshape(BLOCK * BLOCK, -1)
            turned = jnp.dot(turn, block, preferred_element_type=jnp.float32)
            turned = turned.astype(jnp.bfloat16)
            for c in range(BLOCK):
                at = (3 + j0 + c) * height + h0
                xin[pl.ds(at, BLOCK), :] = turned[c * BLOCK : (c + 1) * BLOCK]
    for copy in (*small[1:], *fetches[1:]):
        copy.start()
    fetches[0].wait()

    cells = lax.broadcasted_iota(jnp.int32, routes.shape[1:], 1)
    cells = cells.astype(jnp.float32).astype(jnp.bfloat16)

    def route(j):
        code = jnp.broadcast_to(turned_codes[:, j : j + 1], cells.shape).astype(jnp.bfloat16)
        routes[j] = one_hot(code == cells)

    def interior(src, dst, layer, first, last, beside=None):
        for c in range(first, last, 4 * CH):
            if beside is not None:
                for j in range(c - first, min(c - first + 4 * CH, cols)):
                    beside(j)
            at, size = c * height, (min(c + 4 * CH, last) - c) * height
            dst[pl.ds(at, size), :] = conv_rows(src, [(at, size)], cw, layer, height)

    full = cols // CH
    interior(xin, y1, 0, 3, cols + 1, route)
    pl.semaphore_wait(barrier, 6)

    messages = []

    def send(src, dst, d):
        m = len(messages)
        copy = pltpu.make_async_remote_copy(
            src_ref=src,
            dst_ref=dst,
            send_sem=send_sem.at[m],
            recv_sem=recv_sem.at[m],
            device_id=dev(d),
            device_id_type=pl.DeviceIdType.MESH,
        )
        copy.start()
        messages.append(copy)

    h3 = 3 * height
    send(xin.at[pl.ds(cols * height, h3)], xin.at[pl.ds(0, h3)], 1)
    send(xin.at[pl.ds(h3, h3)], xin.at[pl.ds((cols + 3) * height, h3)], -1)
    for copy in small[1:]:
        copy.wait()
    wdp[0:bins_n, :] = wd[...]
    cot_f = cot[...].astype(jnp.float32)
    for a in range(ba):
        cotwin[pl.ds(cot_own + a * br, br), :] = cot_f[:, a, :].astype(jnp.bfloat16)

    def spread(window, start, edge):
        mine = window.at[pl.ds(start, sec)]
        send(mine, window.at[pl.ds(edge, sec)], 1)
        send(mine, window.at[pl.ds(start + sec, sec)], -1)
        last = window.at[pl.ds(start + sec - edge, edge)]
        send(last, window.at[pl.ds(0, edge)], 2)
        send(window.at[pl.ds(start, edge)], window.at[pl.ds(start + 2 * sec, edge)], -2)

    spread(cotwin, cot_own, br)

    fetches[1].wait()
    interior(y1, y2, 1, 3, cols - 1)
    fetches[2].wait()
    messages[0].wait_recv()
    messages[1].wait_recv()

    def edge(layer, src, dst, extra, done):
        right = (3 + done) * height
        size = (cols + extra) * height - right
        both = conv_rows(src, [(0, h3), (right, size)], cw, layer, height)
        dst[pl.ds(0, h3), :] = both[:h3]
        dst[pl.ds(right, size), :] = both[h3:]

    def middle(i):
        at, size = (3 + 2 * CH * i) * height, 2 * CH * height
        feats[pl.ds(at, size), :] = conv_rows(y2, [(at, size)], cw, 2, height)

    inner = full // 2 - 1
    edge(0, xin, y1, 4, cols - 2)
    for i in range(inner):
        middle(i)
        if i == 0:
            points = counts[...]
            scale = (points > 0).astype(jnp.float32) / jnp.maximum(points, 1).astype(jnp.float32)
            pil = pillars[...].astype(jnp.float32)
            pil = jnp.concatenate(
                [pil[k] * scale[:, k : k + 1] for k in range(2 * br)], axis=0
            ).astype(jnp.bfloat16)
            lb, la = br.bit_length() - 1, ba.bit_length() - 1

            def pillar_row(p):
                r, a, uv = p & (br - 1), (p >> lb) & (ba - 1), p >> (lb + la)
                return ((2 * r + (uv >> 1)) << (la + 1)) + 2 * a + (uv & 1)

            gathered = jnp.dot(
                one_hot_rows(4 * sec, 4 * sec, pillar_row), pil, preferred_element_type=jnp.float32
            ).astype(jnp.bfloat16)
            taps = jnp.concatenate([gathered[k * sec : (k + 1) * sec] for k in range(4)], axis=1)
            lid = jnp.dot(
                taps, lw[...].reshape(taps.shape[1], -1), preferred_element_type=jnp.float32
            )
            lidwin[pl.ds(lid_own, sec), :] = jnp.maximum(lid, 0.0).astype(jnp.bfloat16)
            edge(1, y1, y2, 2, cols - 4)
    edge(2, y2, feats, 0, cols - 2 * CH)
    spread(lidwin, lid_own, 2 * br)
    used = 3 * ba * br
    wide = 2 * CH * height
    lane = lax.broadcasted_iota(jnp.int32, (wide, lanes), 1)

    def soften(at):
        rows = pl.ds(at, wide)
        logits = lax.dot_general(
            feats[rows, :], wdp[...], (((1,), (1,)), ((), ())), preferred_element_type=jnp.float32
        )
        e = jnp.exp(-jnp.abs(logits))
        soft = jnp.maximum(logits, 0.0) + jnp.log(1.0 + e) + 0.05
        soft = jnp.where(lane < bins_n, soft, 0.0)
        inv = 1.0 / jnp.sum(soft, axis=1, keepdims=True)
        p = soft * inv
        probs[rows, :] = p
        slope[rows, :] = logits
        sums[rows, :] = inv
        low[rows, :] = p.astype(jnp.bfloat16)

    def lift(at):
        for row in range(at, at + wide, height):
            rows = pl.ds(row, height)
            a = jnp.dot(low[rows, :], routes[row // height], preferred_element_type=jnp.float32)
            amat[rows, :] = a.astype(jnp.bfloat16)

    soften(0)
    for at in range(0, cols * height, wide):
        if at + wide < cols * height:
            soften(at + wide)
        lift(at)
    mine = lax.dot_general(
        amat[...], feats[...], (((0,), (0,)), ((), ())), preferred_element_type=jnp.float32
    )
    sendbuf[...] = mine.astype(jnp.bfloat16)
    n1, n2, n3 = (2 * ba + 2) * br, (ba + 2) * br, 2 * br
    send(sendbuf.at[pl.ds(used - n1, n1)], rp1, 1)
    send(sendbuf.at[pl.ds(0, n1)], rm1, -1)
    send(sendbuf.at[pl.ds(used - n2, n2)], rp2, 2)
    send(sendbuf.at[pl.ds(0, n2)], rm2, -2)
    send(sendbuf.at[pl.ds(used - n3, n3)], rp3, 3)
    send(sendbuf.at[pl.ds(0, n3)], rm3, -3)
    for at in range(0, cols * height, wide):
        rows = pl.ds(at, wide)
        sig = jax.nn.sigmoid(slope[rows, :]) * sums[rows, :]
        slope[rows, :] = jnp.where(lane < bins_n, sig, 0.0)
    for j in range(0, cols, 2):
        picks[j // 2] = jnp.concatenate(
            [pick_of(row_id, codes, j), pick_of(row_id, codes, j + 1)], axis=1
        )
    for copy in messages[2:10]:
        copy.wait_recv()
    fetches[layers].wait()
    channels = feats.shape[1]
    total = win.shape[0]
    act_rows = total - 2 * br

    def merge(source, lo, hi):
        x = jnp.concatenate([source[i * br : i * br + act_rows] for i in range(3)], axis=1)
        z = [
            jnp.dot(
                x,
                mw[3 * dy : 3 * dy + 3, lo:hi, :].reshape(3 * (hi - lo), -1),
                preferred_element_type=jnp.float32,
            )
            for dy in range(3)
        ]
        return rolled_sum(z[0], z[1], z[2], br)

    lid_act = merge(lidwin[...], channels, mw.shape[1])
    win[pl.ds(2 * br, used), :] = mine
    for copy in messages[10:]:
        copy.wait_recv()
    for got, size in ((rp1, n1), (rp2, n2), (rp3, n3)):
        win[pl.ds(0, size), :] += got[...].astype(jnp.float32)
    for got, size in ((rm1, n1), (rm2, n2), (rm3, n3)):
        win[pl.ds(total - size, size), :] += got[...].astype(jnp.float32)

    act = lid_act + merge(win[...].astype(jnp.bfloat16), 0, channels)
    gate = 1.0 / (1.0 + jnp.exp(-act))
    merged = (act * gate)[cot_own : cot_own + sec]
    merged_o[...] = jnp.stack(
        [merged[a * br : (a + 1) * br] for a in range(ba)], axis=1
    ).astype(jnp.bfloat16)
    grad_pre = (
        cotwin[...].astype(jnp.float32) * (gate * (1.0 + act * (1.0 - gate)))
    ).astype(jnp.bfloat16)

    def merge_back(first, rows, lo, hi):
        y = []
        for dy in range(3):
            acc = None
            for i in range(3):
                term = lax.dot_general(
                    grad_pre[first + (2 - i) * br : first + (2 - i) * br + rows],
                    mw[3 * dy + i, lo:hi, :],
                    (((1,), (1,)), ((), ())),
                    preferred_element_type=jnp.float32,
                )
                acc = term if acc is None else acc + term
            y.append(acc)
        return rolled_sum(y[2], y[1], y[0], br)

    table[...] = merge_back(0, used, 0, channels).astype(jnp.bfloat16)
    lid_grad = merge_back(sec, sec, channels, mw.shape[1])
    lidgrad_o[...] = jnp.stack(
        [lid_grad[a * br : (a + 1) * br] for a in range(ba)], axis=1
    ).astype(jnp.bfloat16)
    for copy in messages:
        copy.wait_send()


def back_kernel(
    height, bins_n, steps,
    feats, amat, probs, slope, picks, table, wd, merged, lid_grad,
    camgrad_o, merged_o, lidgrad_o,
    wdp, seen, gprobs, glog, buf, sem,
):
    lanes = wdp.shape[0]
    copies = [
        pltpu.make_async_copy(merged, merged_o, sem.at[0]),
        pltpu.make_async_copy(lid_grad, lidgrad_o, sem.at[1]),
    ]
    for copy in copies:
        copy.start()
    wdp[...] = jnp.zeros_like(wdp)
    wdp[0:bins_n, :] = wd[...]
    turn = block_turn()
    tab = table[...]
    seen[...] = lax.dot_general(
        feats[...], tab, (((1,), (1,)), ((), ())), preferred_element_type=jnp.float32
    ).astype(jnp.bfloat16)
    for pair in range(picks.shape[0]):
        at = 2 * pair * height
        both = jnp.dot(
            seen[pl.ds(at, 2 * height), :], picks[pair], preferred_element_type=jnp.float32
        )
        gprobs[pl.ds(at, height), :] = both[:height, :lanes]
        gprobs[pl.ds(at + height, height), :] = both[height:, lanes:]
    gp = gprobs[...]
    mean = jnp.sum(gp * probs[...], axis=1, keepdims=True)
    glog[...] = ((gp - mean) * slope[...]).astype(jnp.bfloat16)
    wide = BLOCK * height

    def total(step):
        rows = pl.ds(step * wide, wide)
        direct = jnp.dot(amat[rows, :], tab, preferred_element_type=jnp.float32)
        depth = jnp.dot(glog[rows, :], wdp[...], preferred_element_type=jnp.float32)
        return (direct + depth).astype(jnp.bfloat16)

    blocks = [total(step) for step in range(steps)]
    for k, h0 in enumerate(range(0, height, BLOCK)):
        for step, block in enumerate(blocks):
            part = jnp.concatenate(
                [block[c * height + h0 : c * height + h0 + BLOCK] for c in range(BLOCK)], axis=0
            )
            turned = jnp.dot(turn, part, preferred_element_type=jnp.float32)
            buf[h0 : h0 + BLOCK, pl.ds(step * BLOCK, BLOCK), :] = turned.astype(
                jnp.bfloat16
            ).reshape(BLOCK, BLOCK, -1)
        for q in range(4):
            rows = pl.ds(h0 + q * (BLOCK // 4), BLOCK // 4)
            copy = pltpu.make_async_copy(
                buf.at[rows], camgrad_o.at[rows], sem.at[2 + 4 * k + q]
            )
            copy.start()
            copies.append(copy)
    for copy in copies:
        copy.wait()


def local(
    n, strips,
    image_feats, cam_weights, depth_weight, ray_bins, pillar_sums, pillar_counts,
    lidar_weight, merge_weight, out_cotangent,
):
    height, cols, channels = image_feats.shape
    br, ba, cf = out_cotangent.shape
    bins_n = depth_weight.shape[1]
    cl = pillar_sums.shape[2]
    lanes = -(-bins_n // 128) * 128
    used = groups = 3 * ba * br
    total = (3 * ba + 4) * br
    bf, f32 = jnp.bfloat16, jnp.float32

    vm = pl.BlockSpec(memory_space=pltpu.VMEM)
    hbm = pl.BlockSpec(memory_space=pltpu.HBM)
    n1, n2, n3 = (2 * ba + 2) * br, (ba + 2) * br, 2 * br
    rows = cols * height
    turned_counts = pillar_counts.T
    turned_depth = depth_weight.T
    merged, lid_grad, table, picks, feats, amat, probs, slope = pl.pallas_call(
        functools.partial(kernel, n, strips, cols, height, br, ba, bins_n),
        out_shape=(
            pltpu.VMEM((br, ba, cf), bf),
            pltpu.VMEM((br, ba, cl), bf),
            pltpu.VMEM((groups, channels), bf),
            pltpu.VMEM((cols // 2, groups, 2 * lanes), bf),
            pltpu.VMEM((rows, channels), bf),
            pltpu.VMEM((rows, groups), bf),
            pltpu.VMEM((rows, lanes), f32),
            pltpu.VMEM((rows, lanes), f32),
        ),
        in_specs=[hbm] * 9,
        out_specs=(vm,) * 8,
        scratch_shapes=[
            pltpu.VMEM(image_feats.shape, bf),
            pltpu.VMEM(cam_weights.shape, bf),
            pltpu.VMEM(merge_weight.shape, bf),
            pltpu.VMEM(((cols + 6) * height, channels), bf),
            pltpu.VMEM(((cols + 4) * height, channels), bf),
            pltpu.VMEM(((cols + 2) * height, channels), bf),
            pltpu.VMEM(turned_depth.shape, bf),
            pltpu.VMEM(ray_bins.shape, jnp.int32),
            pltpu.VMEM(pillar_sums.shape, bf),
            pltpu.VMEM(turned_counts.shape, jnp.int32),
            pltpu.VMEM(lidar_weight.shape, bf),
            pltpu.VMEM(out_cotangent.shape, bf),
            pltpu.VMEM((lanes, channels), bf),
            pltpu.VMEM((cols * height, 1), f32),
            pltpu.VMEM((cols * height, lanes), bf),
            pltpu.VMEM((groups, lanes), bf),
            pltpu.VMEM((cols, lanes), f32),
            pltpu.VMEM((cols, lanes, groups), bf),
            pltpu.VMEM((used, channels), bf),
            pltpu.VMEM((n1, channels), bf),
            pltpu.VMEM((n2, channels), bf),
            pltpu.VMEM((n3, channels), bf),
            pltpu.VMEM((n1, channels), bf),
            pltpu.VMEM((n2, channels), bf),
            pltpu.VMEM((n3, channels), bf),
            pltpu.VMEM((total, channels), f32),
            pltpu.VMEM((total, cl), bf),
            pltpu.VMEM((total - 2 * br, cf), bf),
            pltpu.SemaphoreType.DMA((cam_weights.shape[0] + 7,)),
            pltpu.SemaphoreType.DMA((2 * height // BLOCK,)),
            pltpu.SemaphoreType.DMA((16,)),
            pltpu.SemaphoreType.DMA((16,)),
        ],
        compiler_params=pltpu.CompilerParams(
            collective_id=0, has_side_effects=True, vmem_limit_bytes=44 * 1024 * 1024
        ),
        name="bev",
    )(
        *(
            pltpu.with_memory_space_constraint(x, pltpu.HBM)
            for x in (
                image_feats, cam_weights, turned_depth, ray_bins, pillar_sums, turned_counts,
                lidar_weight, out_cotangent, merge_weight,
            )
        )
    )
    steps = cols // BLOCK
    cam_grad, merged, lid_grad = pl.pallas_call(
        functools.partial(back_kernel, height, bins_n, steps),
        out_shape=(
            pltpu.HBM((height, cols, channels), bf),
            pltpu.HBM((br, ba, cf), bf),
            pltpu.HBM((br, ba, cl), bf),
        ),
        in_specs=[vm] * 9,
        out_specs=(hbm,) * 3,
        scratch_shapes=[
            pltpu.VMEM((lanes, channels), bf),
            pltpu.VMEM((rows, groups), bf),
            pltpu.VMEM((rows, lanes), f32),
            pltpu.VMEM((rows, lanes), bf),
            pltpu.VMEM((height, cols, channels), bf),
            pltpu.SemaphoreType.DMA((2 + 4 * (height // BLOCK),)),
        ],
        compiler_params=pltpu.CompilerParams(vmem_limit_bytes=20 * 1024 * 1024),
        name="back",
    )(feats, amat, probs, slope, picks, table, turned_depth, merged, lid_grad)
    return merged, cam_grad, lid_grad


def solution(mesh):
    strips = mesh.shape["strip"]
    n = mesh.shape["branch"] * strips
    placed = (
        P(None, AXES, None),
        P(),
        P(),
        P(AXES, None),
        P(None, AXES, None),
        P(None, AXES),
        P(),
        P(),
        P(None, AXES, None),
    )
    return jax.shard_map(
        functools.partial(local, n, strips),
        mesh=mesh,
        in_specs=placed,
        out_specs=(P(None, AXES, None),) * 3,
        check_vma=False,
    )
```

```python
import functools

import jax
import jax.numpy as jnp
from jax import lax
from jax.experimental import pallas as pl
from jax.experimental.pallas import tpu as pltpu
from jax.sharding import PartitionSpec as P

AXES = ("branch", "strip")
CH = 8
BLOCK = 16


def rolled_sum(low, mid, high, period):
    rows = mid.shape[0]
    place = lax.broadcasted_iota(jnp.int32, mid.shape, 0) & (period - 1)
    down = jnp.where(place == 0, 0.0, pltpu.roll(low, 1, 0))
    up = jnp.where(place == period - 1, 0.0, pltpu.roll(high, rows - 1, 0))
    return mid + down + up


def conv_rows(src, pieces, weights, layer, height):
    taps = [
        jnp.concatenate([src[pl.ds(s + i * height, rows), :] for s, rows in pieces], axis=0)
        for i in range(3)
    ]
    x = jnp.concatenate(taps, axis=1)
    channels = taps[0].shape[1]
    z = [
        jnp.dot(
            x,
            weights[layer, 3 * dy : 3 * dy + 3].reshape(3 * channels, -1),
            preferred_element_type=jnp.float32,
        )
        for dy in range(3)
    ]
    total = rolled_sum(z[0], z[1], z[2], height)
    return jnp.maximum(total, 0.0).astype(jnp.bfloat16)


def one_hot_rows(rows, sources, source_of):
    p = lax.broadcasted_iota(jnp.int32, (rows, sources), 0)
    q = lax.broadcasted_iota(jnp.int32, (rows, sources), 1)
    return jnp.where(source_of(p) == q, 1.0, 0.0).astype(jnp.bfloat16)


def row_numbers(shape):
    return lax.broadcasted_iota(jnp.int32, shape, 0).astype(jnp.float32).astype(jnp.bfloat16)


def one_hot(hit):
    return jnp.where(hit, jnp.ones((), jnp.bfloat16), jnp.zeros((), jnp.bfloat16))


def pick_of(row_id, codes, j):
    groups, lanes = row_id.shape
    code = jnp.broadcast_to(codes[pl.ds(j, 1), :], (16, lanes)).astype(jnp.bfloat16)
    code = jnp.concatenate([code] * (groups // 16), axis=0)
    return one_hot(row_id[...] == code)


def block_turn():
    shift = BLOCK.bit_length() - 1
    return one_hot_rows(
        BLOCK * BLOCK,
        BLOCK * BLOCK,
        lambda p: ((p & (BLOCK - 1)) << shift) + (p >> shift),
    )


def kernel(
    n, strips, cols, height, br, ba, bins_n,
    img_hbm, cw_hbm, wd_hbm, bins_hbm, pillars_hbm, counts_hbm, lw_hbm, cot_hbm, mw_hbm,
    merged_o, lidgrad_o, table, picks, feats, amat, probs, slope,
    img, cw, mw, xin, y1, y2, wd, bins, pillars, counts, lw, cot,
    wdp, sums, low, row_id, codes, routes, sendbuf,
    rp1, rp2, rp3, rm1, rm2, rm3, win, lidwin, cotwin,
    local_sem, image_sem, send_sem, recv_sem,
):
    me = lax.axis_index(AXES[0]) * strips + lax.axis_index(AXES[1])
    ch_rows = CH * height
    lanes = wdp.shape[0]

    def dev(d):
        t = lax.rem(me + d + n, n)
        return (t // strips, t % strips)

    barrier = pltpu.get_barrier_semaphore()
    for d in (1, 2, 3, -1, -2, -3):
        pl.semaphore_signal(
            barrier, inc=1, device_id=dev(d), device_id_type=pl.DeviceIdType.MESH
        )
    layers = cw.shape[0]
    blocks = range(0, height, BLOCK)
    half = BLOCK // 2
    chunks = [
        pltpu.make_async_copy(img_hbm.at[pl.ds(h0, half)], img.at[pl.ds(h0, half)], image_sem.at[i])
        for i, h0 in enumerate(range(0, height, half))
    ]
    fetches = [
        pltpu.make_async_copy(cw_hbm.at[k], cw.at[k], local_sem.at[k]) for k in range(layers)
    ]
    fetches.append(pltpu.make_async_copy(mw_hbm, mw, local_sem.at[layers]))
    small = [
        pltpu.make_async_copy(src, dst, local_sem.at[layers + 1 + i])
        for i, (src, dst) in enumerate(
            (
                (bins_hbm, bins), (pillars_hbm, pillars), (counts_hbm, counts), (lw_hbm, lw),
                (cot_hbm, cot), (wd_hbm, wd),
            )
        )
    ]
    for copy in (*chunks, small[0], fetches[0]):
        copy.start()
    row_id[...] = row_numbers(row_id.shape)
    wdp[...] = jnp.zeros_like(wdp)
    codes[...] = jnp.full(codes.shape, -1.0, jnp.float32)
    win[...] = jnp.zeros_like(win)
    sec = ba * br
    cot_own, lid_own = (ba + 1) * br, (ba + 2) * br
    small[0].wait()
    cell = br * ba
    sh_cell, sh_ba, sh_br = cell.bit_length() - 1, ba.bit_length() - 1, br.bit_length() - 1
    raw = bins[...]
    off = (raw >> sh_cell) - me + 1
    off = jnp.where(off < 0, off + n, off)
    off = jnp.where(off >= n, off - n, off)
    in_cell = raw & (cell - 1)
    code = (((off << sh_ba) + (in_cell & (ba - 1))) << sh_br) + (in_cell >> sh_ba)
    codes[:, 0:bins_n] = code.astype(jnp.float32)
    turned_codes = jnp.transpose(codes[...])
    turn = block_turn()
    for i, h0 in enumerate(blocks):
        chunks[2 * i].wait()
        chunks[2 * i + 1].wait()
        for j0 in range(0, cols, BLOCK):
            block = img[h0 : h0 + BLOCK, j0 : j0 + BLOCK, :].reshape(BLOCK * BLOCK, -1)
            turned = jnp.dot(turn, block, preferred_element_type=jnp.float32)
            turned = turned.astype(jnp.bfloat16)
            for c in range(BLOCK):
                at = (3 + j0 + c) * height + h0
                xin[pl.ds(at, BLOCK), :] = turned[c * BLOCK : (c + 1) * BLOCK]
    for copy in (*small[1:], *fetches[1:]):
        copy.start()
    fetches[0].wait()

    cells = lax.broadcasted_iota(jnp.int32, routes.shape[1:], 1)
    cells = cells.astype(jnp.float32).astype(jnp.bfloat16)

    def route(j):
        code = jnp.broadcast_to(turned_codes[:, j : j + 1], cells.shape).astype(jnp.bfloat16)
        routes[j] = one_hot(code == cells)

    def interior(src, dst, layer, first, last, beside=None):
        for c in range(first, last, 4 * CH):
            if beside is not None:
                for j in range(c - first, min(c - first + 4 * CH, cols)):
                    beside(j)
            at, size = c * height, (min(c + 4 * CH, last) - c) * height
            dst[pl.ds(at, size), :] = conv_rows(src, [(at, size)], cw, layer, height)

    full = cols // CH
    interior(xin, y1, 0, 3, cols + 1, route)
    pl.semaphore_wait(barrier, 6)

    messages = []

    def send(src, dst, d):
        m = len(messages)
        copy = pltpu.make_async_remote_copy(
            src_ref=src,
            dst_ref=dst,
            send_sem=send_sem.at[m],
            recv_sem=recv_sem.at[m],
            device_id=dev(d),
            device_id_type=pl.DeviceIdType.MESH,
        )
        copy.start()
        messages.append(copy)

    h3 = 3 * height
    send(xin.at[pl.ds(cols * height, h3)], xin.at[pl.ds(0, h3)], 1)
    send(xin.at[pl.ds(h3, h3)], xin.at[pl.ds((cols + 3) * height, h3)], -1)
    for copy in small[1:]:
        copy.wait()
    wdp[0:bins_n, :] = wd[...]
    cot_f = cot[...].astype(jnp.float32)
    for a in range(ba):
        cotwin[pl.ds(cot_own + a * br, br), :] = cot_f[:, a, :].astype(jnp.bfloat16)

    def spread(window, start, edge):
        mine = window.at[pl.ds(start, sec)]
        send(mine, window.at[pl.ds(edge, sec)], 1)
        send(mine, window.at[pl.ds(start + sec, sec)], -1)
        last = window.at[pl.ds(start + sec - edge, edge)]
        send(last, window.at[pl.ds(0, edge)], 2)
        send(window.at[pl.ds(start, edge)], window.at[pl.ds(start + 2 * sec, edge)], -2)

    spread(cotwin, cot_own, br)

    fetches[1].wait()
    interior(y1, y2, 1, 3, cols - 1)
    fetches[2].wait()
    messages[0].wait_recv()
    messages[1].wait_recv()
    used = 3 * ba * br
    wide = 2 * CH * height
    lane = lax.broadcasted_iota(jnp.int32, (wide, lanes), 1)

    def soften(at):
        rows = pl.ds(at, wide)
        logits = lax.dot_general(
            feats[rows, :], wdp[...], (((1,), (1,)), ((), ())), preferred_element_type=jnp.float32
        )
        e = jnp.exp(-jnp.abs(logits))
        soft = jnp.maximum(logits, 0.0) + jnp.log(1.0 + e) + 0.05
        soft = jnp.where(lane < bins_n, soft, 0.0)
        inv = 1.0 / jnp.sum(soft, axis=1, keepdims=True)
        p = soft * inv
        probs[rows, :] = p
        slope[rows, :] = logits
        sums[rows, :] = inv
        low[rows, :] = p.astype(jnp.bfloat16)

    def lift(at):
        for row in range(at, at + wide, height):
            rows = pl.ds(row, height)
            a = jnp.dot(low[rows, :], routes[row // height], preferred_element_type=jnp.float32)
            amat[rows, :] = a.astype(jnp.bfloat16)


    def edge(layer, src, dst, extra, done):
        right = (3 + done) * height
        size = (cols + extra) * height - right
        both = conv_rows(src, [(0, h3), (right, size)], cw, layer, height)
        dst[pl.ds(0, h3), :] = both[:h3]
        dst[pl.ds(right, size), :] = both[h3:]

    def middle(i):
        at, size = (3 + 2 * CH * i) * height, 2 * CH * height
        feats[pl.ds(at, size), :] = conv_rows(y2, [(at, size)], cw, 2, height)

    inner = full // 2 - 1
    edge(0, xin, y1, 4, cols - 2)
    for i in range(inner):
        middle(i)
        if i == 0:
            points = counts[...]
            scale = (points > 0).astype(jnp.float32) / jnp.maximum(points, 1).astype(jnp.float32)
            pil = pillars[...].astype(jnp.float32)
            pil = jnp.concatenate(
                [pil[k] * scale[:, k : k + 1] for k in range(2 * br)], axis=0
            ).astype(jnp.bfloat16)
            lb, la = br.bit_length() - 1, ba.bit_length() - 1

            def pillar_row(p):
                r, a, uv = p & (br - 1), (p >> lb) & (ba - 1), p >> (lb + la)
                return ((2 * r + (uv >> 1)) << (la + 1)) + 2 * a + (uv & 1)

            gathered = jnp.dot(
                one_hot_rows(4 * sec, 4 * sec, pillar_row), pil, preferred_element_type=jnp.float32
            ).astype(jnp.bfloat16)
            taps = jnp.concatenate([gathered[k * sec : (k + 1) * sec] for k in range(4)], axis=1)
            lid = jnp.dot(
                taps, lw[...].reshape(taps.shape[1], -1), preferred_element_type=jnp.float32
            )
            lidwin[pl.ds(lid_own, sec), :] = jnp.maximum(lid, 0.0).astype(jnp.bfloat16)
            edge(1, y1, y2, 2, cols - 4)
        else:
            soften(i * wide)
    edge(2, y2, feats, 0, cols - 2 * CH)
    early = [i * wide for i in range(1, inner)]
    late = [at for at in range(0, cols * height, wide) if at not in early]
    for at in early:
        lift(at)
    for at in late:
        soften(at)
    for at in late:
        lift(at)
    spread(lidwin, lid_own, 2 * br)
    mine = lax.dot_general(
        amat[...], feats[...], (((0,), (0,)), ((), ())), preferred_element_type=jnp.float32
    )
    sendbuf[...] = mine.astype(jnp.bfloat16)
    n1, n2, n3 = (2 * ba + 2) * br, (ba + 2) * br, 2 * br
    send(sendbuf.at[pl.ds(used - n1, n1)], rp1, 1)
    send(sendbuf.at[pl.ds(0, n1)], rm1, -1)
    send(sendbuf.at[pl.ds(used - n2, n2)], rp2, 2)
    send(sendbuf.at[pl.ds(0, n2)], rm2, -2)
    send(sendbuf.at[pl.ds(used - n3, n3)], rp3, 3)
    send(sendbuf.at[pl.ds(0, n3)], rm3, -3)
    for at in range(0, cols * height, wide):
        rows = pl.ds(at, wide)
        sig = jax.nn.sigmoid(slope[rows, :]) * sums[rows, :]
        slope[rows, :] = jnp.where(lane < bins_n, sig, 0.0)
    for j in range(0, cols, 2):
        picks[j // 2] = jnp.concatenate(
            [pick_of(row_id, codes, j), pick_of(row_id, codes, j + 1)], axis=1
        )
    for copy in messages[2:10]:
        copy.wait_recv()
    fetches[layers].wait()
    channels = feats.shape[1]
    total = win.shape[0]
    act_rows = total - 2 * br

    def merge(source, lo, hi):
        x = jnp.concatenate([source[i * br : i * br + act_rows] for i in range(3)], axis=1)
        z = [
            jnp.dot(
                x,
                mw[3 * dy : 3 * dy + 3, lo:hi, :].reshape(3 * (hi - lo), -1),
                preferred_element_type=jnp.float32,
            )
            for dy in range(3)
        ]
        return rolled_sum(z[0], z[1], z[2], br)

    lid_act = merge(lidwin[...], channels, mw.shape[1])
    win[pl.ds(2 * br, used), :] = mine
    for copy in messages[10:]:
        copy.wait_recv()
    for got, size in ((rp1, n1), (rp2, n2), (rp3, n3)):
        win[pl.ds(0, size), :] += got[...].astype(jnp.float32)
    for got, size in ((rm1, n1), (rm2, n2), (rm3, n3)):
        win[pl.ds(total - size, size), :] += got[...].astype(jnp.float32)

    act = lid_act + merge(win[...].astype(jnp.bfloat16), 0, channels)
    gate = 1.0 / (1.0 + jnp.exp(-act))
    merged = (act * gate)[cot_own : cot_own + sec]
    merged_o[...] = jnp.stack(
        [merged[a * br : (a + 1) * br] for a in range(ba)], axis=1
    ).astype(jnp.bfloat16)
    grad_pre = (
        cotwin[...].astype(jnp.float32) * (gate * (1.0 + act * (1.0 - gate)))
    ).astype(jnp.bfloat16)

    def merge_back(first, rows, lo, hi):
        y = []
        for dy in range(3):
            acc = None
            for i in range(3):
                term = lax.dot_general(
                    grad_pre[first + (2 - i) * br : first + (2 - i) * br + rows],
                    mw[3 * dy + i, lo:hi, :],
                    (((1,), (1,)), ((), ())),
                    preferred_element_type=jnp.float32,
                )
                acc = term if acc is None else acc + term
            y.append(acc)
        return rolled_sum(y[2], y[1], y[0], br)

    table[...] = merge_back(0, used, 0, channels).astype(jnp.bfloat16)
    lid_grad = merge_back(sec, sec, channels, mw.shape[1])
    lidgrad_o[...] = jnp.stack(
        [lid_grad[a * br : (a + 1) * br] for a in range(ba)], axis=1
    ).astype(jnp.bfloat16)
    for copy in messages:
        copy.wait_send()


def back_kernel(
    height, bins_n, steps,
    feats, amat, probs, slope, picks, table, wd, merged, lid_grad,
    camgrad_o, merged_o, lidgrad_o,
    wdp, seen, gprobs, glog, buf, sem,
):
    lanes = wdp.shape[0]
    copies = [
        pltpu.make_async_copy(merged, merged_o, sem.at[0]),
        pltpu.make_async_copy(lid_grad, lidgrad_o, sem.at[1]),
    ]
    for copy in copies:
        copy.start()
    wdp[...] = jnp.zeros_like(wdp)
    wdp[0:bins_n, :] = wd[...]
    turn = block_turn()
    tab = table[...]
    seen[...] = lax.dot_general(
        feats[...], tab, (((1,), (1,)), ((), ())), preferred_element_type=jnp.float32
    ).astype(jnp.bfloat16)
    for pair in range(picks.shape[0]):
        at = 2 * pair * height
        both = jnp.dot(
            seen[pl.ds(at, 2 * height), :], picks[pair], preferred_element_type=jnp.float32
        )
        gprobs[pl.ds(at, height), :] = both[:height, :lanes]
        gprobs[pl.ds(at + height, height), :] = both[height:, lanes:]
    gp = gprobs[...]
    mean = jnp.sum(gp * probs[...], axis=1, keepdims=True)
    glog[...] = ((gp - mean) * slope[...]).astype(jnp.bfloat16)
    wide = BLOCK * height

    def total(step):
        rows = pl.ds(step * wide, wide)
        direct = jnp.dot(amat[rows, :], tab, preferred_element_type=jnp.float32)
        depth = jnp.dot(glog[rows, :], wdp[...], preferred_element_type=jnp.float32)
        return (direct + depth).astype(jnp.bfloat16)

    blocks = [total(step) for step in range(steps)]
    for k, h0 in enumerate(range(0, height, BLOCK)):
        for step, block in enumerate(blocks):
            part = jnp.concatenate(
                [block[c * height + h0 : c * height + h0 + BLOCK] for c in range(BLOCK)], axis=0
            )
            turned = jnp.dot(turn, part, preferred_element_type=jnp.float32)
            buf[h0 : h0 + BLOCK, pl.ds(step * BLOCK, BLOCK), :] = turned.astype(
                jnp.bfloat16
            ).reshape(BLOCK, BLOCK, -1)
        for q in range(4):
            rows = pl.ds(h0 + q * (BLOCK // 4), BLOCK // 4)
            copy = pltpu.make_async_copy(
                buf.at[rows], camgrad_o.at[rows], sem.at[2 + 4 * k + q]
            )
            copy.start()
            copies.append(copy)
    for copy in copies:
        copy.wait()


def local(
    n, strips,
    image_feats, cam_weights, depth_weight, ray_bins, pillar_sums, pillar_counts,
    lidar_weight, merge_weight, out_cotangent,
):
    height, cols, channels = image_feats.shape
    br, ba, cf = out_cotangent.shape
    bins_n = depth_weight.shape[1]
    cl = pillar_sums.shape[2]
    lanes = -(-bins_n // 128) * 128
    used = groups = 3 * ba * br
    total = (3 * ba + 4) * br
    bf, f32 = jnp.bfloat16, jnp.float32

    vm = pl.BlockSpec(memory_space=pltpu.VMEM)
    hbm = pl.BlockSpec(memory_space=pltpu.HBM)
    n1, n2, n3 = (2 * ba + 2) * br, (ba + 2) * br, 2 * br
    rows = cols * height
    turned_counts = pillar_counts.T
    turned_depth = depth_weight.T
    merged, lid_grad, table, picks, feats, amat, probs, slope = pl.pallas_call(
        functools.partial(kernel, n, strips, cols, height, br, ba, bins_n),
        out_shape=(
            pltpu.VMEM((br, ba, cf), bf),
            pltpu.VMEM((br, ba, cl), bf),
            pltpu.VMEM((groups, channels), bf),
            pltpu.VMEM((cols // 2, groups, 2 * lanes), bf),
            pltpu.VMEM((rows, channels), bf),
            pltpu.VMEM((rows, groups), bf),
            pltpu.VMEM((rows, lanes), f32),
            pltpu.VMEM((rows, lanes), f32),
        ),
        in_specs=[hbm] * 9,
        out_specs=(vm,) * 8,
        scratch_shapes=[
            pltpu.VMEM(image_feats.shape, bf),
            pltpu.VMEM(cam_weights.shape, bf),
            pltpu.VMEM(merge_weight.shape, bf),
            pltpu.VMEM(((cols + 6) * height, channels), bf),
            pltpu.VMEM(((cols + 4) * height, channels), bf),
            pltpu.VMEM(((cols + 2) * height, channels), bf),
            pltpu.VMEM(turned_depth.shape, bf),
            pltpu.VMEM(ray_bins.shape, jnp.int32),
            pltpu.VMEM(pillar_sums.shape, bf),
            pltpu.VMEM(turned_counts.shape, jnp.int32),
            pltpu.VMEM(lidar_weight.shape, bf),
            pltpu.VMEM(out_cotangent.shape, bf),
            pltpu.VMEM((lanes, channels), bf),
            pltpu.VMEM((cols * height, 1), f32),
            pltpu.VMEM((cols * height, lanes), bf),
            pltpu.VMEM((groups, lanes), bf),
            pltpu.VMEM((cols, lanes), f32),
            pltpu.VMEM((cols, lanes, groups), bf),
            pltpu.VMEM((used, channels), bf),
            pltpu.VMEM((n1, channels), bf),
            pltpu.VMEM((n2, channels), bf),
            pltpu.VMEM((n3, channels), bf),
            pltpu.VMEM((n1, channels), bf),
            pltpu.VMEM((n2, channels), bf),
            pltpu.VMEM((n3, channels), bf),
            pltpu.VMEM((total, channels), f32),
            pltpu.VMEM((total, cl), bf),
            pltpu.VMEM((total - 2 * br, cf), bf),
            pltpu.SemaphoreType.DMA((cam_weights.shape[0] + 7,)),
            pltpu.SemaphoreType.DMA((2 * height // BLOCK,)),
            pltpu.SemaphoreType.DMA((16,)),
            pltpu.SemaphoreType.DMA((16,)),
        ],
        compiler_params=pltpu.CompilerParams(
            collective_id=0, has_side_effects=True, vmem_limit_bytes=44 * 1024 * 1024
        ),
        name="bev",
    )(
        *(
            pltpu.with_memory_space_constraint(x, pltpu.HBM)
            for x in (
                image_feats, cam_weights, turned_depth, ray_bins, pillar_sums, turned_counts,
                lidar_weight, out_cotangent, merge_weight,
            )
        )
    )
    steps = cols // BLOCK
    cam_grad, merged, lid_grad = pl.pallas_call(
        functools.partial(back_kernel, height, bins_n, steps),
        out_shape=(
            pltpu.HBM((height, cols, channels), bf),
            pltpu.HBM((br, ba, cf), bf),
            pltpu.HBM((br, ba, cl), bf),
        ),
        in_specs=[vm] * 9,
        out_specs=(hbm,) * 3,
        scratch_shapes=[
            pltpu.VMEM((lanes, channels), bf),
            pltpu.VMEM((rows, groups), bf),
            pltpu.VMEM((rows, lanes), f32),
            pltpu.VMEM((rows, lanes), bf),
            pltpu.VMEM((height, cols, channels), bf),
            pltpu.SemaphoreType.DMA((2 + 4 * (height // BLOCK),)),
        ],
        compiler_params=pltpu.CompilerParams(vmem_limit_bytes=20 * 1024 * 1024),
        name="back",
    )(feats, amat, probs, slope, picks, table, turned_depth, merged, lid_grad)
    return merged, cam_grad, lid_grad


def solution(mesh):
    strips = mesh.shape["strip"]
    n = mesh.shape["branch"] * strips
    placed = (
        P(None, AXES, None),
        P(),
        P(),
        P(AXES, None),
        P(None, AXES, None),
        P(None, AXES),
        P(),
        P(),
        P(None, AXES, None),
    )
    return jax.shard_map(
        functools.partial(local, n, strips),
        mesh=mesh,
        in_specs=placed,
        out_specs=(P(None, AXES, None),) * 3,
        check_vma=False,
    )
```
